32 devices in a mesh: row: 4 (over z), col: 8 (over y, x, core).
Axes of the slice: x: 2, y: 2, z: 4, core: 2. Of those that a mesh axis runs over, the one named last changes fastest.
Arguments:
- velocity: bfloat16 [3, 8, 2048, 2048], P(None, 'col', 'row'), may hold values from -6 to 6
- vorticity: bfloat16 [3, 8, 2048, 2048], P(None, 'col', 'row'), may hold values from -6 to 6
- eddy_state: bfloat16 [8, 64, 3072], P('col', 'row'), may hold values from -0.359375 to 0.359375
- eddy_rate: bfloat16 [8, 64], P('col', 'row'), may hold values from 8 to 64
- block_owner: int32 [8, 4, 64, 1], P('col', 'row'), may hold values from 0 to 3; in each aligned block of 64 rows (0 to 63, 64 to 127, ..., all dimensions but the last counted through in order) at most 32 rows name the same one
- block_slot: int32 [8, 4, 64], P('col', 'row'), may hold values from 0 to 15
Outputs:
- spectral: float32 [3, 8, 1638400], P(None, None, ('row', 'col'))
The draws below stay inside these ranges and needn't reach their ends.
Inputs may be any that keep to these rules, and one draw needn't show every extreme that they name: `block_owner`: among the 64 blocks of one DNS device, at most 32 have the same owner.
All inputs are finite; a program needn't handle non-finite values.
Results may differ from the reference program's by a relative error of at most 0.013.
Values may be sent and summed in bfloat16 or wider, within the bound.
A program may use at most 128 MiB of HBM per device.

```python
import math
import jax
import jax.numpy as jnp
import numpy as np
from jax import lax

NX = 2048
NY = 2048
KXM = 640
KYM = 1280
RATIO = 4
BY = 8
BX = 128
S = 16
ZD = 1
ZW = 8
XC = 512
YC = 128
NB = 64
BLKV = 3072
CAP = 32
KXD = 160
KYD = 160
MODES = 1638400
N_ROW = 4
N_COL = 8


def with_ends(values, key, low, largest):
    extent = values.shape
    place = [jax.random.randint(jax.random.fold_in(key, axis), (), 0, extent[axis]) for axis in range(len(extent))]
    values = values.at[tuple(place)].set(low)
    longest = extent.index(max(extent))
    place[longest] = (place[longest] + 1) % extent[longest]
    return values.at[tuple(place)].set(largest)


def block_scale(key, extent, split, smallest, top_value):
    loudness, own = 1.0, jax.random.fold_in(key, 6)
    for dim, blocks in split:
        draws = jnp.exp(jax.random.uniform(jax.random.fold_in(own, dim), (blocks,), jnp.float32, smallest / len(split), top_value / len(split)))
        loudness = loudness * jnp.repeat(draws, extent[dim] // blocks).reshape([-1 if axis == dim else 1 for axis in range(len(extent))])
    return loudness


def deal_out(stream_key, own, number, rows, count, top, reach, lean):
    ranking = jax.random.permutation(stream_key, count)
    packed, common = load_shares(count, rows * top, reach, lean, True), load_shares(count, rows * top, reach, lean, False)
    places = jnp.arange(count)

    def named(tallies, offset_by):
        used = int((tallies > 0).sum())
        fixed = max(1, used // 4)
        passed = fixed + (places - fixed + offset_by * (used - fixed)) % max(1, count - fixed)
        return jnp.zeros((count,), jnp.int32).at[ranking[jnp.where(places < fixed, places, passed)]].set(jnp.asarray(tallies, jnp.int32))

    tallies = jnp.where(number % 4 == 0, named(packed, number // 4), named(common, number - number // 4 - 1))
    mixed = jax.random.permutation(jax.random.fold_in(own, 3), count)
    giver, receiver = mixed[0:count // 2 * 2:2], mixed[1:count // 2 * 2:2]
    slack = jnp.minimum(tallies[giver] - 1, reach - tallies[receiver]) // 2
    slack = jnp.where((giver == ranking[0]) | (receiver == ranking[0]) | (tallies[receiver] == 0), 0, jnp.maximum(slack, 0))
    passed = jax.random.randint(jax.random.fold_in(own, 4), (count // 2,), 0, 1 << 20) % (slack + 1)
    tallies = tallies.at[giver].add(-passed).at[receiver].add(passed)
    items = jnp.searchsorted(jnp.cumsum(tallies), jnp.arange(rows * top), side="right").astype(jnp.int32)
    listing = items.reshape(top, rows).T
    listing = listing[jax.random.permutation(jax.random.fold_in(own, 1), rows)]
    offset_by = jax.random.randint(jax.random.fold_in(own, 2), (rows, 1), 0, top)
    return jnp.take_along_axis(listing, (jnp.arange(top)[None, :] + offset_by) % top, axis=1)


def load_shares(amount, total, most, slope, full):
    portions = [(1 << 20) // math.isqrt(rank ** slope) + 1 for rank in range(1, amount + 1)]
    largest = most if full else min(most, max(-(-total // amount), total * portions[0] // sum(portions)))
    least = 1 if total - largest >= amount - 1 else 0
    holding, spare = [largest] + [least] * (amount - 1), total - largest - least * (amount - 1)
    while spare > 0:
        free = [i for i in range(1, amount) if holding[i] < largest] or [i for i in range(1, amount) if holding[i] < most]
        pool, left = sum([portions[i] for i in free]), spare
        for i in free:
            addition = min(most - holding[i], max(1, left * portions[i] // pool), spare)
            holding[i] = holding[i] + addition
            spare = spare - addition
    return np.array(holding)


def bell_draw(own_key, shape, deviation, most, cuts=(), kind=jnp.bfloat16):
    gain = block_scale(own_key, shape, cuts, -0.22, 0.18) if cuts else 1.0
    values = jax.random.normal(own_key, shape, jnp.float32) * deviation * gain
    return jnp.minimum(jnp.maximum(values, -most), most).astype(kind)


def setup_inputs(seed: int = 0) -> dict:
    key_list = jax.random.split(jax.random.key(seed), 7)
    velocity = bell_draw(key_list[0], (3, ZW, NY, NX), 1.0, 6.0, ((1, 8), (2, 4)))
    vorticity = bell_draw(key_list[1], (3, ZW, NY, NX), 1.0, 6.0, ((1, 8), (2, 4)))
    eddy_state = bell_draw(key_list[2], (N_COL, N_ROW * S, BLKV), 0.06, 0.359375, ((0, 8), (1, 4)))
    eddy_rate = jnp.clip(jnp.exp(math.log(64.0) - 2.0794415 * jax.random.uniform(key_list[3], (N_COL, N_ROW * S), jnp.float32) ** block_scale(key_list[3], (N_COL, N_ROW * S), ((0, 8), (1, 4)), -0.2, 0.2)), 8.0, 64.0).astype(jnp.bfloat16)
    block_owner_keys = jax.random.split(jax.random.fold_in(key_list[4], 1), N_COL * N_ROW * NB // NB)
    block_owner_turns = jax.random.permutation(jax.random.fold_in(key_list[4], 3), N_COL * N_ROW * NB // NB)
    block_owner = jax.vmap(lambda own, number: deal_out(jax.random.fold_in(key_list[4], 2), own, number, NB, N_ROW, 1, CAP, 2))(block_owner_keys, block_owner_turns).reshape((N_COL, N_ROW, NB, 1))
    block_slot = with_ends(jax.random.randint(key_list[5], (N_COL, N_ROW, NB), 0, S), jax.random.fold_in(key_list[5], 1), 0, S - 1).astype(jnp.int32)
    return {"velocity": velocity, "vorticity": vorticity, "eddy_state": eddy_state, "eddy_rate": eddy_rate, "block_owner": block_owner, "block_slot": block_slot}


section_step = 0.5
viscous_step = 0.15
vertical_step = 0.5

def gauss_value(position, ratio):
    spread = 4.0 * ratio * ratio
    taps = jnp.arange(5 * ratio).astype(jnp.float32)
    shifted = taps - 2.0 * ratio - (ratio - 1) / 2.0
    total = jnp.sum(jnp.exp(-shifted * shifted / (2.0 * spread)))
    moved = position - 2.0 * ratio - (ratio - 1) / 2.0
    return jnp.exp(-moved * moved / (2.0 * spread)) / total

def x_weights(points, coarse, ratio):
    fine = jnp.arange(points, dtype=jnp.int32)[:, None]
    cells = jnp.arange(coarse, dtype=jnp.int32)[None, :]
    offset = jnp.mod(fine - ratio * cells + 2 * ratio, points)
    value = gauss_value(offset.astype(jnp.float32), ratio)
    return jnp.where(offset < 5 * ratio, value, 0.0).astype(jnp.bfloat16)

def x_table(points, kept):
    fine = jnp.arange(points, dtype=jnp.int32)[:, None]
    column = jnp.arange(2 * kept, dtype=jnp.int32)[None, :]
    phase = jnp.mod(column // 2 * fine, points).astype(jnp.float32) * (2.0 * math.pi / points)
    value = jnp.where(column % 2 == 0, jnp.cos(phase), -jnp.sin(phase))
    return (value / math.sqrt(points)).astype(jnp.bfloat16)

def y_tables(points, kept, first, count):
    fine = jnp.arange(points, dtype=jnp.int32)[:, None]
    wave = jnp.arange(count, dtype=jnp.int32)[None, :] + (first - kept // 2)
    phase = jnp.mod(wave * fine, points).astype(jnp.float32) * (2.0 * math.pi / points)
    scale = 1.0 / math.sqrt(points)
    return ((jnp.cos(phase) * scale).astype(jnp.bfloat16), (jnp.sin(phase) * scale).astype(jnp.bfloat16))

def vertical_inverse(planes):
    index = jnp.arange(planes)
    ends = (index == 0) | (index == planes - 1)
    diagonal = jnp.where(ends, 1.0 + vertical_step, 1.0 + 2.0 * vertical_step).astype(jnp.float32)
    lower = jnp.where(index == 0, 0.0, -vertical_step).astype(jnp.float32)
    upper = jnp.where(index == planes - 1, 0.0, -vertical_step).astype(jnp.float32)
    return lax.linalg.tridiagonal_solve(lower, diagonal, upper, jnp.eye(planes, dtype=jnp.float32))

def damping(x_wave, y_wave, points_x, points_y):
    angle_x = x_wave.astype(jnp.float32) * (2.0 * math.pi / points_x)
    angle_y = y_wave.astype(jnp.float32) * (2.0 * math.pi / points_y)
    total = angle_y[:, None, None] * angle_y[:, None, None] + angle_x[None, None, :] * angle_x[None, None, :]
    return jnp.broadcast_to(jnp.exp(-viscous_step * total), (y_wave.shape[0], 2, x_wave.shape[0]))

def reference(velocity, vorticity, eddy_state, eddy_rate, block_owner, block_slot):
    highest = lax.Precision.HIGHEST
    xweights = x_weights(NX, XC, RATIO).astype(jnp.float32)
    taps = gauss_value(jnp.arange(5 * RATIO).astype(jnp.float32), RATIO)
    taps = lax.optimization_barrier(taps.astype(jnp.bfloat16)).astype(jnp.float32)
    xtable = x_table(NX, KXM).astype(jnp.float32)
    ycos, ysin = y_tables(NY, KYM, 0, KYM)
    ycos = ycos.astype(jnp.float32)
    ysin = ysin.astype(jnp.float32)

    def filter_plane(index):
        plane = lax.dynamic_index_in_dim(velocity, index, 1, keepdims=False).astype(jnp.float32)
        along = jnp.dot(plane.reshape(3 * NY, NX).astype(jnp.float32), xweights.astype(jnp.float32), precision=highest, preferred_element_type=jnp.float32).reshape(3, NY, XC)
        along = lax.optimization_barrier(along.astype(jnp.bfloat16)).astype(jnp.float32)
        total = jnp.zeros((3, NY // RATIO, XC), jnp.float32)
        for tap in range(5 * RATIO):
            moved = jnp.roll(along, 2 * RATIO - tap, axis=1)
            total = total + taps[tap] * moved[:, ::RATIO, :]
        return total.astype(jnp.bfloat16)
    filtered = lax.map(filter_plane, jnp.arange(ZW, dtype=jnp.int32))
    blocks = filtered.reshape(N_COL, ZD, 3, N_ROW, YC // BY, BY, XC // BX, BX)
    blocks = blocks.transpose(0, 3, 1, 4, 6, 2, 5, 7).reshape(N_COL, N_ROW * NB, BLKV)
    owners = block_owner.reshape(N_COL, N_ROW * NB).astype(jnp.int32)
    slots = block_slot.reshape(N_COL, N_ROW * NB).astype(jnp.int32)
    chosen = (owners * S + slots).astype(jnp.int32)
    state = jnp.take_along_axis(eddy_state, chosen[:, :, None], axis=1).astype(jnp.float32)
    rates = jnp.take_along_axis(eddy_rate, chosen, axis=1).astype(jnp.float32)
    forcing_blocks = (rates[:, :, None] * (state - blocks.astype(jnp.float32))).astype(jnp.bfloat16)
    coarse = forcing_blocks.reshape(N_COL, N_ROW, ZD, YC // BY, XC // BX, 3, BY, BX)
    coarse = coarse.transpose(0, 2, 5, 1, 3, 6, 4, 7).reshape(ZW, 3, NY // RATIO, XC)

    def transform_plane(index):
        speed = lax.dynamic_index_in_dim(velocity, index, 1, keepdims=False).astype(jnp.float32)
        spin = lax.dynamic_index_in_dim(vorticity, index, 1, keepdims=False).astype(jnp.float32)
        local = lax.dynamic_index_in_dim(coarse, index, 0, keepdims=False).astype(jnp.float32)
        forcing = jnp.repeat(jnp.repeat(local, RATIO, axis=1), RATIO, axis=2)
        cross = jnp.stack([speed[1] * spin[2] - speed[2] * spin[1], speed[2] * spin[0] - speed[0] * spin[2], speed[0] * spin[1] - speed[1] * spin[0]], axis=0)
        section = (speed + section_step * (cross + forcing)).astype(jnp.bfloat16)
        xspec = jnp.dot(section.reshape(3 * NY, NX).astype(jnp.float32), xtable.astype(jnp.float32), precision=highest, preferred_element_type=jnp.float32).astype(jnp.bfloat16)
        xspec = xspec.reshape(3, NY, KXM, 2).astype(jnp.float32)
        real_in = xspec[:, :, :, 0]
        imag_in = xspec[:, :, :, 1]
        real_out = jnp.einsum('cnk,nj->cjk', real_in, ycos, precision=highest) + jnp.einsum('cnk,nj->cjk', imag_in, ysin, precision=highest)
        imag_out = jnp.einsum('cnk,nj->cjk', imag_in, ycos, precision=highest) - jnp.einsum('cnk,nj->cjk', real_in, ysin, precision=highest)
        return jnp.stack([real_out, imag_out], axis=2).astype(jnp.bfloat16)
    spectrum = lax.map(transform_plane, jnp.arange(ZW, dtype=jnp.int32))
    inverse = vertical_inverse(ZW).astype(jnp.bfloat16).astype(jnp.float32)
    mixed = jnp.einsum('wz,zcjpk->cwjpk', inverse, spectrum.astype(jnp.float32), precision=highest)
    factor = damping(jnp.arange(KXM), jnp.arange(KYM) - KYM // 2, NX, NY)
    result = mixed * factor[None, None]
    result = result.reshape(3, ZW, N_COL, KYD, 2, N_ROW, KXD).transpose(0, 1, 5, 2, 3, 4, 6)
    return result.reshape(3, ZW, MODES)
```

```python
import math

import jax
import jax.numpy as jnp
import numpy as np
from jax import lax
from jax.experimental import pallas as pl
from jax.experimental.pallas import tpu as pltpu
from jax.sharding import PartitionSpec as P

NX = 2048
NY = 2048
KXM = 640
KYM = 1280
RATIO = 4
BY = 8
BX = 128
S = 16
BLKV = 3072


section_step = 0.5
viscous_step = 0.15
vertical_step = 0.5


def padded_2(cells, sides, width):
    for axis, dim in sides:
        count = lax.axis_size(axis)
        head = lax.slice_in_dim(cells, 0, width, axis=dim)
        tail = lax.slice_in_dim(cells, cells.shape[dim] - width, cells.shape[dim], axis=dim)
        cells = jnp.concatenate(
            [
                lax.ppermute(tail, axis, [(i, (i + 1) % count) for i in range(count)]),
                cells,
                lax.ppermute(head, axis, [((i + 1) % count, i) for i in range(count)]),
            ],
            axis=dim,
        )
    return cells


def gauss_value(position, ratio):
    spread = 4.0 * ratio * ratio
    taps = jnp.arange(5 * ratio).astype(jnp.float32)
    shifted = taps - 2.0 * ratio - (ratio - 1) / 2.0
    total = jnp.sum(jnp.exp(-shifted * shifted / (2.0 * spread)))
    moved = position - 2.0 * ratio - (ratio - 1) / 2.0
    return jnp.exp(-moved * moved / (2.0 * spread)) / total


def x_weights(points, coarse, ratio):
    fine = jnp.arange(points, dtype=jnp.int32)[:, None]
    cells = jnp.arange(coarse, dtype=jnp.int32)[None, :]
    offset = jnp.mod(fine - ratio * cells + 2 * ratio, points)
    value = gauss_value(offset.astype(jnp.float32), ratio)
    return jnp.where(offset < 5 * ratio, value, 0.0).astype(jnp.bfloat16)


def y_weights(coarse, padded, ratio):
    cells = jnp.arange(coarse, dtype=jnp.int32)[:, None]
    fine = jnp.arange(padded, dtype=jnp.int32)[None, :]
    offset = fine - ratio * cells
    value = gauss_value(offset.astype(jnp.float32), ratio)
    return jnp.where((offset >= 0) & (offset < 5 * ratio), value, 0.0).astype(jnp.bfloat16)


def x_table(points, kept):
    fine = jnp.arange(points, dtype=jnp.int32)[:, None]
    column = jnp.arange(2 * kept, dtype=jnp.int32)[None, :]
    phase = jnp.mod(column // 2 * fine, points).astype(jnp.float32) * (2.0 * math.pi / points)
    value = jnp.where(column % 2 == 0, jnp.cos(phase), -jnp.sin(phase))
    return (value / math.sqrt(points)).astype(jnp.bfloat16)


def y_tables(points, kept, first, count):
    fine = jnp.arange(points, dtype=jnp.int32)[:, None]
    wave = jnp.arange(count, dtype=jnp.int32)[None, :] + (first - kept // 2)
    phase = jnp.mod(wave * fine, points).astype(jnp.float32) * (2.0 * math.pi / points)
    scale = 1.0 / math.sqrt(points)
    return (
        (jnp.cos(phase) * scale).astype(jnp.bfloat16),
        (jnp.sin(phase) * scale).astype(jnp.bfloat16),
    )


def vertical_inverse(planes):
    index = jnp.arange(planes)
    ends = (index == 0) | (index == planes - 1)
    diagonal = jnp.where(ends, 1.0 + vertical_step, 1.0 + 2.0 * vertical_step).astype(jnp.float32)
    lower = jnp.where(index == 0, 0.0, -vertical_step).astype(jnp.float32)
    upper = jnp.where(index == planes - 1, 0.0, -vertical_step).astype(jnp.float32)
    return lax.linalg.tridiagonal_solve(lower, diagonal, upper, jnp.eye(planes, dtype=jnp.float32))


def damping(x_wave, y_wave, points_x, points_y):
    angle_x = x_wave.astype(jnp.float32) * (2.0 * math.pi / points_x)
    angle_y = y_wave.astype(jnp.float32) * (2.0 * math.pi / points_y)
    total = (
        angle_y[:, None, None] * angle_y[:, None, None]
        + angle_x[None, None, :] * angle_x[None, None, :]
    )
    return jnp.broadcast_to(jnp.exp(-viscous_step * total), (y_wave.shape[0], 2, x_wave.shape[0]))


def along_y(piece):
    items, width, length = piece.shape
    half = width // 2
    split = piece.reshape(items, half, 2, length)
    real_in = split[:, :, 0, :]
    imag_in = split[:, :, 1, :]
    block = 256
    outputs = []
    for first in range(0, KYM, block):
        cosine, sine = y_tables(length, KYM, first, block)
        real_out = jnp.einsum(
            "kin,nj->kji", real_in, cosine, preferred_element_type=jnp.float32
        ) + jnp.einsum("kin,nj->kji", imag_in, sine, preferred_element_type=jnp.float32)
        imag_out = jnp.einsum(
            "kin,nj->kji", imag_in, cosine, preferred_element_type=jnp.float32
        ) - jnp.einsum("kin,nj->kji", real_in, sine, preferred_element_type=jnp.float32)
        outputs.append(jnp.concatenate([real_out, imag_out], axis=2))
    return jnp.concatenate(outputs, axis=1).astype(jnp.bfloat16)


def generic_device(velocity, vorticity, eddy_state, eddy_rate, block_owner, block_slot):
    components, depth, rows, points = velocity.shape
    coarse_rows = rows // RATIO
    coarse_cols = points // RATIO
    xweights = x_weights(points, coarse_cols, RATIO)
    local = jnp.einsum(
        "czyn,nx->czyx", velocity, xweights, preferred_element_type=jnp.float32
    ).astype(jnp.bfloat16)
    along = padded_2(local, (("row", 2),), 2 * RATIO)
    yweights = y_weights(coarse_rows, rows + 4 * RATIO, RATIO)
    filtered = jnp.einsum(
        "iy,czyx->czix", yweights, along, preferred_element_type=jnp.float32
    ).astype(jnp.bfloat16)
    ybands = coarse_rows // BY
    xbands = coarse_cols // BX
    count = depth * ybands * xbands
    blocks = filtered.reshape(components, depth, ybands, BY, xbands, BX).transpose(1, 2, 4, 0, 3, 5)
    blocks = blocks.reshape(count, BLKV)
    owners = block_owner.reshape(count)
    slots = block_slot.reshape(count)
    owners_total = lax.axis_size("row")
    every_state, every_rate = (
        lax.all_gather(eddy_state, "row", axis=1, tiled=True),
        lax.all_gather(eddy_rate, "row", axis=1, tiled=True),
    )
    chosen = owners * S + slots
    lookup = (chosen[:, None] == jnp.arange(owners_total * S, dtype=jnp.int32)[None, :]).astype(
        jnp.bfloat16
    )
    state = jnp.dot(lookup, every_state[0], preferred_element_type=jnp.float32)
    rates = jnp.dot(lookup, every_rate[0][:, None], preferred_element_type=jnp.float32)[:, 0]
    forcing_blocks = (rates[:, None] * (state - blocks.astype(jnp.float32))).astype(jnp.bfloat16)
    coarse = forcing_blocks.reshape(depth, ybands, xbands, components, BY, BX).transpose(
        3, 0, 1, 4, 2, 5
    )
    coarse = coarse.reshape(components, depth, coarse_rows, coarse_cols).astype(jnp.float32)
    forcing = jnp.repeat(jnp.repeat(coarse, RATIO, axis=2), RATIO, axis=3)
    speed = velocity.astype(jnp.float32)
    spin = vorticity.astype(jnp.float32)
    cross = jnp.stack(
        [
            speed[1] * spin[2] - speed[2] * spin[1],
            speed[2] * spin[0] - speed[0] * spin[2],
            speed[0] * spin[1] - speed[1] * spin[0],
        ],
        axis=0,
    )
    section = (speed + section_step * (cross + forcing)).astype(jnp.bfloat16)
    xtable = x_table(points, KXM)
    spectrum = jnp.einsum(
        "kyn,nm->kmy",
        section.reshape(components * depth, rows, points),
        xtable,
        preferred_element_type=jnp.float32,
    ).astype(jnp.bfloat16)
    ordered = along_y(lax.all_to_all(spectrum, "row", split_axis=1, concat_axis=2, tiled=True))
    ordered = ordered.reshape(components, depth, KYM, -1)
    inverse = vertical_inverse(depth * lax.axis_size("col")).astype(jnp.bfloat16)
    mode_rows = KYM // lax.axis_size("col")
    mode_cols = ordered.shape[3] // 2
    x_wave = lax.axis_index("row") * mode_cols + jnp.arange(mode_cols, dtype=jnp.int32)
    y_wave = lax.axis_index("col") * mode_rows + jnp.arange(mode_rows, dtype=jnp.int32) - KYM // 2
    factor = damping(x_wave, y_wave, NX, NY).reshape(-1)
    piece = lax.all_to_all(ordered, "col", split_axis=2, concat_axis=1, tiled=True)
    items = piece.shape[0]
    flat = piece.reshape(items, piece.shape[1], -1)
    mixed = jnp.einsum("wz,kzl->kwl", inverse, flat, preferred_element_type=jnp.float32)
    return mixed * factor[None, None, :]


F32 = jnp.float32
BF16 = jnp.bfloat16
YB = 256
NT = (((1,), (1,)), ((), ()))


def fits(rows, points, n_row, n_col):
    mode_cols, mode_rows = KXM // n_row, KYM // n_col
    return (
        n_row == 4
        and rows % YB == 0
        and points % 512 == 0
        and mode_cols % 16 == 0
        and (2 * mode_cols) % 128 == 64
        and mode_rows % 32 == 0
        and n_col % 8 == 0
    )


def x_tables_t(points, kept, n_row):
    per = kept // n_row
    row = np.arange(2 * kept)
    wave = row // (2 * per) * per + row % per
    imag = row // per % 2
    phase = (wave[:, None] * np.arange(points)[None, :]) % points * (2.0 * math.pi / points)
    value = np.where(imag[:, None] == 0, np.cos(phase), -np.sin(phase)) / math.sqrt(points)
    fine = value.astype(BF16)
    coarse = section_step * fine.astype(np.float32).reshape(2 * kept, points // RATIO, RATIO).sum(2)
    return fine, coarse.astype(BF16)


def y_tables_t(points, kept, quarter):
    s = np.arange(kept // 4)
    out = []
    for q in range(4):
        wave = 4 * s + q - kept // 2
        phase = (wave[:, None] * np.arange(quarter)[None, :]) % points * (2.0 * math.pi / points)
        out.append(np.concatenate([np.cos(phase), np.sin(phase)], axis=1) / math.sqrt(points))
    return np.stack(out).astype(BF16)


def x_kernel(comp, vel_ref, vort_ref, coarse_ref, xt_ref, xc_ref, out_ref):
    b, c = (comp + 1) % 3, (comp + 2) % 3
    section = (
        vel_ref[comp].astype(F32)
        + section_step
        * (
            vel_ref[b].astype(F32) * vort_ref[c].astype(F32)
            - vel_ref[c].astype(F32) * vort_ref[b].astype(F32)
        )
    ).astype(BF16)
    yb = section.shape[0]
    fine = lax.broadcasted_iota(jnp.int32, (yb, yb // RATIO), 0) // RATIO
    cell = lax.broadcasted_iota(jnp.int32, (yb, yb // RATIO), 1)
    spread = jnp.where(fine == cell, 1.0, 0.0).astype(BF16)
    repeated = jnp.dot(spread, coarse_ref[0], preferred_element_type=F32).astype(BF16)
    dests, width, _ = out_ref.shape
    for r in range(dests):
        lines = slice(r * width, (r + 1) * width)
        total = lax.dot_general(xt_ref[lines, :], section, NT, preferred_element_type=F32)
        total += lax.dot_general(xc_ref[lines, :], repeated, NT, preferred_element_type=F32)
        out_ref[r] = total.astype(BF16)


def x_stage(comp, vel, vort, coarse, xt, xc, n_row):
    _, rows, points = vel.shape
    width = xt.shape[0] // n_row
    full = lambda a: pl.BlockSpec(a.shape, lambda i: (0,) * a.ndim)
    return pl.pallas_call(
        lambda *refs: x_kernel(comp, *refs),
        out_shape=jax.ShapeDtypeStruct((n_row, width, rows), BF16),
        grid=(rows // YB,),
        in_specs=[
            pl.BlockSpec((3, YB, points), lambda i: (0, i, 0)),
            pl.BlockSpec((3, YB, points), lambda i: (0, i, 0)),
            pl.BlockSpec((1, YB // RATIO, points // RATIO), lambda i: (comp, i, 0)),
            full(xt),
            full(xc),
        ],
        out_specs=pl.BlockSpec((n_row, width, YB), lambda i: (0, 0, i)),
        cost_estimate=pl.CostEstimate(
            flops=2 * rows * xt.shape[0] * (points + points // RATIO),
            bytes_accessed=20 * rows * points,
            transcendentals=0,
        ),
        compiler_params=pltpu.CompilerParams(vmem_limit_bytes=56 * 2**20),
        name="x_stage",
    )(vel, vort, coarse, xt, xc)


def y_kernel(in_ref, tab_ref, out_ref):
    half = in_ref.shape[1] // 2
    a = [in_ref[r, :half, :].astype(F32) for r in range(4)]
    b = [in_ref[r, half:, :].astype(F32) for r in range(4)]
    a02, a13, b02, b13 = a[0] + a[2], a[1] + a[3], b[0] + b[2], b[1] + b[3]
    d02, d13, e02, e13 = a[0] - a[2], a[1] - a[3], b[0] - b[2], b[1] - b[3]
    real = [a02 + a13, d02 + e13, a02 - a13, d02 - e13]
    imag = [b02 + b13, e02 - d13, b02 - b13, e02 + d13]
    results = []
    for q in range(4):
        re, im = real[q].astype(BF16), imag[q].astype(BF16)
        turned = jnp.concatenate(
            [jnp.concatenate([re, im], axis=0), jnp.concatenate([im, -re], axis=0)], axis=1
        )
        results.append(lax.dot_general(tab_ref[q], turned, NT, preferred_element_type=F32))
    dests, lines, _ = out_ref.shape
    part = lines // 4
    for d in range(dests):
        out_ref[d] = jnp.concatenate(
            [results[q][d * part : (d + 1) * part] for q in range(4)], axis=0
        ).astype(BF16)


def y_stage(piece, tab, n_col):
    _, width, quarter = piece.shape
    lines = 4 * tab.shape[1] // n_col
    return pl.pallas_call(
        y_kernel,
        out_shape=jax.ShapeDtypeStruct((n_col, lines, width), BF16),
        cost_estimate=pl.CostEstimate(
            flops=2 * tab.size * width, bytes_accessed=8 * tab.size, transcendentals=0
        ),
        compiler_params=pltpu.CompilerParams(vmem_limit_bytes=40 * 2**20),
        name="y_stage",
    )(piece, tab)


def z_kernel(in_ref, mix_ref, factor_ref, *rest):
    out_ref, held = rest[-2:]
    planes, lines, width = in_ref.shape
    part = lines // 4
    for blk in range(lines // 16):
        cut = slice(blk * 16, (blk + 1) * 16)
        group = in_ref[:, cut, :].reshape(planes * 16, width)
        mixed = jnp.dot(mix_ref[...], group, preferred_element_type=F32)
        held[cut] = mixed.reshape(16, planes, width)

    def body(s, carry):
        for pair in range(2):
            left = held[2 * pair * part + s]
            right = held[(2 * pair + 1) * part + s]
            lanes = pl.ds(pl.multiple_of((2 * s + pair) * 2 * width, 128), 2 * width)
            out_ref[0, :, lanes] = jnp.concatenate([left, right], axis=1) * factor_ref[:, lanes]
        return carry

    lax.fori_loop(0, part, body, 0)


def z_stage(comp, piece, mix, factor, before):
    planes, lines, width = piece.shape
    whole = lambda a: pl.BlockSpec(a.shape, lambda i: (0,) * a.ndim)
    args = [piece, mix, factor]
    specs = [whole(a) for a in args]
    aliases = {}
    if before is not None:
        aliases = {3: 0}
        args.append(before)
        specs.append(pl.BlockSpec(memory_space=pl.ANY))
    return pl.pallas_call(
        z_kernel,
        out_shape=jax.ShapeDtypeStruct((3, planes, lines * width), F32),
        grid=(1,),
        in_specs=specs,
        out_specs=pl.BlockSpec((1, planes, lines * width), lambda i: (comp, 0, 0)),
        scratch_shapes=[pltpu.VMEM((lines, planes, width), F32)],
        input_output_aliases=aliases,
        compiler_params=pltpu.CompilerParams(vmem_limit_bytes=40 * 2**20),
        name="z_stage",
    )(*args)


def coarse_forcing(velocity, eddy_state, eddy_rate, block_owner, block_slot):
    components, depth, rows, points = velocity.shape
    coarse_rows = rows // RATIO
    coarse_cols = points // RATIO
    xweights = x_weights(points, coarse_cols, RATIO)
    local = jnp.einsum(
        "czyn,nx->czyx", velocity, xweights, preferred_element_type=jnp.float32
    ).astype(jnp.bfloat16)
    along = padded_2(local, (("row", 2),), 2 * RATIO)
    yweights = y_weights(coarse_rows, rows + 4 * RATIO, RATIO)
    filtered = jnp.einsum(
        "iy,czyx->czix", yweights, along, preferred_element_type=jnp.float32
    ).astype(jnp.bfloat16)
    ybands = coarse_rows // BY
    xbands = coarse_cols // BX
    count = depth * ybands * xbands
    blocks = filtered.reshape(components, depth, ybands, BY, xbands, BX).transpose(1, 2, 4, 0, 3, 5)
    blocks = blocks.reshape(count, BLKV)
    owners = block_owner.reshape(count)
    slots = block_slot.reshape(count)
    owners_total = lax.axis_size("row")
    every_state, every_rate = (
        lax.all_gather(eddy_state, "row", axis=1, tiled=True),
        lax.all_gather(eddy_rate, "row", axis=1, tiled=True),
    )
    chosen = owners * S + slots
    lookup = (chosen[:, None] == jnp.arange(owners_total * S, dtype=jnp.int32)[None, :]).astype(
        jnp.bfloat16
    )
    state = jnp.dot(lookup, every_state[0], preferred_element_type=jnp.float32)
    rates = jnp.dot(lookup, every_rate[0][:, None], preferred_element_type=jnp.float32)[:, 0]
    forcing_blocks = (rates[:, None] * (state - blocks.astype(jnp.float32))).astype(jnp.bfloat16)
    coarse = forcing_blocks.reshape(depth, ybands, xbands, components, BY, BX).transpose(
        3, 0, 1, 4, 2, 5
    )
    return coarse.reshape(components, coarse_rows, coarse_cols)


def per_device(velocity, vorticity, eddy_state, eddy_rate, block_owner, block_slot):
    components, depth, rows, points = velocity.shape
    n_row, n_col = lax.axis_size("row"), lax.axis_size("col")
    if depth != 1 or not fits(rows, points, n_row, n_col):
        return generic_device(velocity, vorticity, eddy_state, eddy_rate, block_owner, block_slot)
    coarse = coarse_forcing(velocity, eddy_state, eddy_rate, block_owner, block_slot)
    vel = velocity.reshape(components, rows, points)
    vort = vorticity.reshape(components, rows, points)
    xt, xc = (jnp.asarray(t) for t in x_tables_t(points, KXM, n_row))
    tab = jnp.asarray(y_tables_t(rows * n_row, KYM, rows))
    planes = depth * n_col
    inverse = vertical_inverse(planes).astype(jnp.bfloat16)
    eye = jnp.eye(16, dtype=BF16)
    mix = (eye[:, None, None, :] * inverse[None, :, :, None]).reshape(16 * planes, planes * 16)
    mode_rows = KYM // n_col
    mode_cols = KXM // n_row
    x_wave = lax.axis_index("row") * mode_cols + jnp.arange(mode_cols, dtype=jnp.int32)
    y_wave = lax.axis_index("col") * mode_rows + jnp.arange(mode_rows, dtype=jnp.int32) - KYM // 2
    factor = damping(x_wave, y_wave, NX, NY).reshape(1, -1)
    result = None
    spectra = [x_stage(c, vel, vort, coarse, xt, xc, n_row) for c in range(components)]
    pieces = [lax.all_to_all(s, "row", split_axis=0, concat_axis=0, tiled=True) for s in spectra]
    ordered = [y_stage(p, tab, n_col) for p in pieces]
    columns = [lax.all_to_all(o, "col", split_axis=0, concat_axis=0, tiled=True) for o in ordered]
    for c in range(components):
        result = z_stage(c, columns[c], mix, factor, result)
    return result


def solution(mesh):
    return jax.shard_map(
        per_device,
        mesh=mesh,
        in_specs=(
            P(None, "col", "row", None),
            P(None, "col", "row", None),
            P("col", "row", None),
            P("col", "row"),
            P("col", "row", None, None),
            P("col", "row", None),
        ),
        out_specs=P(None, None, ("row", "col")),
        check_vma=False,
    )
```

```python
import math

import jax
import jax.numpy as jnp
import numpy as np
from jax import lax
from jax.experimental import pallas as pl
from jax.experimental.pallas import tpu as pltpu
from jax.sharding import PartitionSpec as P

NX = 2048
NY = 2048
KXM = 640
KYM = 1280
RATIO = 4
BY = 8
BX = 128
S = 16
BLKV = 3072


section_step = 0.5
viscous_step = 0.15
vertical_step = 0.5


def padded_2(cells, sides, width):
    for axis, dim in sides:
        count = lax.axis_size(axis)
        head = lax.slice_in_dim(cells, 0, width, axis=dim)
        tail = lax.slice_in_dim(cells, cells.shape[dim] - width, cells.shape[dim], axis=dim)
        cells = jnp.concatenate(
            [
                lax.ppermute(tail, axis, [(i, (i + 1) % count) for i in range(count)]),
                cells,
                lax.ppermute(head, axis, [((i + 1) % count, i) for i in range(count)]),
            ],
            axis=dim,
        )
    return cells


def gauss_value(position, ratio):
    spread = 4.0 * ratio * ratio
    taps = jnp.arange(5 * ratio).astype(jnp.float32)
    shifted = taps - 2.0 * ratio - (ratio - 1) / 2.0
    total = jnp.sum(jnp.exp(-shifted * shifted / (2.0 * spread)))
    moved = position - 2.0 * ratio - (ratio - 1) / 2.0
    return jnp.exp(-moved * moved / (2.0 * spread)) / total


def x_weights(points, coarse, ratio):
    fine = jnp.arange(points, dtype=jnp.int32)[:, None]
    cells = jnp.arange(coarse, dtype=jnp.int32)[None, :]
    offset = jnp.mod(fine - ratio * cells + 2 * ratio, points)
    value = gauss_value(offset.astype(jnp.float32), ratio)
    return jnp.where(offset < 5 * ratio, value, 0.0).astype(jnp.bfloat16)


def y_weights(coarse, padded, ratio):
    cells = jnp.arange(coarse, dtype=jnp.int32)[:, None]
    fine = jnp.arange(padded, dtype=jnp.int32)[None, :]
    offset = fine - ratio * cells
    value = gauss_value(offset.astype(jnp.float32), ratio)
    return jnp.where((offset >= 0) & (offset < 5 * ratio), value, 0.0).astype(jnp.bfloat16)


def x_table(points, kept):
    fine = jnp.arange(points, dtype=jnp.int32)[:, None]
    column = jnp.arange(2 * kept, dtype=jnp.int32)[None, :]
    phase = jnp.mod(column // 2 * fine, points).astype(jnp.float32) * (2.0 * math.pi / points)
    value = jnp.where(column % 2 == 0, jnp.cos(phase), -jnp.sin(phase))
    return (value / math.sqrt(points)).astype(jnp.bfloat16)


def y_tables(points, kept, first, count):
    fine = jnp.arange(points, dtype=jnp.int32)[:, None]
    wave = jnp.arange(count, dtype=jnp.int32)[None, :] + (first - kept // 2)
    phase = jnp.mod(wave * fine, points).astype(jnp.float32) * (2.0 * math.pi / points)
    scale = 1.0 / math.sqrt(points)
    return (
        (jnp.cos(phase) * scale).astype(jnp.bfloat16),
        (jnp.sin(phase) * scale).astype(jnp.bfloat16),
    )


def vertical_inverse(planes):
    index = jnp.arange(planes)
    ends = (index == 0) | (index == planes - 1)
    diagonal = jnp.where(ends, 1.0 + vertical_step, 1.0 + 2.0 * vertical_step).astype(jnp.float32)
    lower = jnp.where(index == 0, 0.0, -vertical_step).astype(jnp.float32)
    upper = jnp.where(index == planes - 1, 0.0, -vertical_step).astype(jnp.float32)
    return lax.linalg.tridiagonal_solve(lower, diagonal, upper, jnp.eye(planes, dtype=jnp.float32))


def damping(x_wave, y_wave, points_x, points_y):
    angle_x = x_wave.astype(jnp.float32) * (2.0 * math.pi / points_x)
    angle_y = y_wave.astype(jnp.float32) * (2.0 * math.pi / points_y)
    total = (
        angle_y[:, None, None] * angle_y[:, None, None]
        + angle_x[None, None, :] * angle_x[None, None, :]
    )
    return jnp.broadcast_to(jnp.exp(-viscous_step * total), (y_wave.shape[0], 2, x_wave.shape[0]))


def along_y(piece):
    items, width, length = piece.shape
    half = width // 2
    split = piece.reshape(items, half, 2, length)
    real_in = split[:, :, 0, :]
    imag_in = split[:, :, 1, :]
    block = 256
    outputs = []
    for first in range(0, KYM, block):
        cosine, sine = y_tables(length, KYM, first, block)
        real_out = jnp.einsum(
            "kin,nj->kji", real_in, cosine, preferred_element_type=jnp.float32
        ) + jnp.einsum("kin,nj->kji", imag_in, sine, preferred_element_type=jnp.float32)
        imag_out = jnp.einsum(
            "kin,nj->kji", imag_in, cosine, preferred_element_type=jnp.float32
        ) - jnp.einsum("kin,nj->kji", real_in, sine, preferred_element_type=jnp.float32)
        outputs.append(jnp.concatenate([real_out, imag_out], axis=2))
    return jnp.concatenate(outputs, axis=1).astype(jnp.bfloat16)


def generic_device(velocity, vorticity, eddy_state, eddy_rate, block_owner, block_slot):
    components, depth, rows, points = velocity.shape
    coarse_rows = rows // RATIO
    coarse_cols = points // RATIO
    xweights = x_weights(points, coarse_cols, RATIO)
    local = jnp.einsum(
        "czyn,nx->czyx", velocity, xweights, preferred_element_type=jnp.float32
    ).astype(jnp.bfloat16)
    along = padded_2(local, (("row", 2),), 2 * RATIO)
    yweights = y_weights(coarse_rows, rows + 4 * RATIO, RATIO)
    filtered = jnp.einsum(
        "iy,czyx->czix", yweights, along, preferred_element_type=jnp.float32
    ).astype(jnp.bfloat16)
    ybands = coarse_rows // BY
    xbands = coarse_cols // BX
    count = depth * ybands * xbands
    blocks = filtered.reshape(components, depth, ybands, BY, xbands, BX).transpose(1, 2, 4, 0, 3, 5)
    blocks = blocks.reshape(count, BLKV)
    owners = block_owner.reshape(count)
    slots = block_slot.reshape(count)
    owners_total = lax.axis_size("row")
    every_state, every_rate = (
        lax.all_gather(eddy_state, "row", axis=1, tiled=True),
        lax.all_gather(eddy_rate, "row", axis=1, tiled=True),
    )
    chosen = owners * S + slots
    lookup = (chosen[:, None] == jnp.arange(owners_total * S, dtype=jnp.int32)[None, :]).astype(
        jnp.bfloat16
    )
    state = jnp.dot(lookup, every_state[0], preferred_element_type=jnp.float32)
    rates = jnp.dot(lookup, every_rate[0][:, None], preferred_element_type=jnp.float32)[:, 0]
    forcing_blocks = (rates[:, None] * (state - blocks.astype(jnp.float32))).astype(jnp.bfloat16)
    coarse = forcing_blocks.reshape(depth, ybands, xbands, components, BY, BX).transpose(
        3, 0, 1, 4, 2, 5
    )
    coarse = coarse.reshape(components, depth, coarse_rows, coarse_cols).astype(jnp.float32)
    forcing = jnp.repeat(jnp.repeat(coarse, RATIO, axis=2), RATIO, axis=3)
    speed = velocity.astype(jnp.float32)
    spin = vorticity.astype(jnp.float32)
    cross = jnp.stack(
        [
            speed[1] * spin[2] - speed[2] * spin[1],
            speed[2] * spin[0] - speed[0] * spin[2],
            speed[0] * spin[1] - speed[1] * spin[0],
        ],
        axis=0,
    )
    section = (speed + section_step * (cross + forcing)).astype(jnp.bfloat16)
    xtable = x_table(points, KXM)
    spectrum = jnp.einsum(
        "kyn,nm->kmy",
        section.reshape(components * depth, rows, points),
        xtable,
        preferred_element_type=jnp.float32,
    ).astype(jnp.bfloat16)
    ordered = along_y(lax.all_to_all(spectrum, "row", split_axis=1, concat_axis=2, tiled=True))
    ordered = ordered.reshape(components, depth, KYM, -1)
    inverse = vertical_inverse(depth * lax.axis_size("col")).astype(jnp.bfloat16)
    mode_rows = KYM // lax.axis_size("col")
    mode_cols = ordered.shape[3] // 2
    x_wave = lax.axis_index("row") * mode_cols + jnp.arange(mode_cols, dtype=jnp.int32)
    y_wave = lax.axis_index("col") * mode_rows + jnp.arange(mode_rows, dtype=jnp.int32) - KYM // 2
    factor = damping(x_wave, y_wave, NX, NY).reshape(-1)
    piece = lax.all_to_all(ordered, "col", split_axis=2, concat_axis=1, tiled=True)
    items = piece.shape[0]
    flat = piece.reshape(items, piece.shape[1], -1)
    mixed = jnp.einsum("wz,kzl->kwl", inverse, flat, preferred_element_type=jnp.float32)
    return mixed * factor[None, None, :]


MESH = pl.DeviceIdType.MESH
F32 = jnp.float32
BF16 = jnp.bfloat16
YB = 256
NT = (((1,), (1,)), ((), ()))


def fits(rows, points, n_row, n_col):
    mode_cols, mode_rows = KXM // n_row, KYM // n_col
    return (
        n_row == 4
        and rows % YB == 0
        and points % 512 == 0
        and mode_cols % 16 == 0
        and (2 * mode_cols) % 128 == 64
        and mode_rows % 32 == 0
        and n_col == 8
    )


def x_tables_t(points, kept, n_row):
    per = kept // n_row
    row = np.arange(2 * kept)
    wave = row // (2 * per) * per + row % per
    imag = row // per % 2
    phase = (wave[:, None] * np.arange(points)[None, :]) % points * (2.0 * math.pi / points)
    value = np.where(imag[:, None] == 0, np.cos(phase), -np.sin(phase)) / math.sqrt(points)
    fine = value.astype(BF16)
    coarse = section_step * fine.astype(np.float32).reshape(2 * kept, points // RATIO, RATIO).sum(2)
    return fine, coarse.astype(BF16)


def y_tables_t(points, kept, quarter):
    s = np.arange(kept // 4)
    out = []
    for q in range(4):
        wave = 4 * s + q - kept // 2
        phase = (wave[:, None] * np.arange(quarter)[None, :]) % points * (2.0 * math.pi / points)
        out.append(np.concatenate([np.cos(phase), np.sin(phase)], axis=1) / math.sqrt(points))
    return np.stack(out).astype(BF16)


def all_kernel(
    vel, vort, coarse, xt, xc, tab, mix, out,
    velv, vortv, coarsev, xtv, xcv, tabv, section, repeated, xsend, xrecv, ysend, yrecv, held, done,
    load_sem, xs_sem, xr_sem, ys_sem, yr_sem, out_sem,
):
    me, mc = lax.axis_index("row"), lax.axis_index("col")
    n_row, n_col = 4, yrecv.shape[1]
    _, rows, points = velv.shape
    width = xsend.shape[2]
    barrier = pltpu.get_barrier_semaphore()
    for d in range(1, n_row):
        pl.semaphore_signal(
            barrier, inc=1, device_id={"row": lax.rem(me + d, n_row)}, device_id_type=MESH
        )
    for d in range(1, n_col):
        pl.semaphore_signal(
            barrier, inc=1, device_id={"col": lax.rem(mc + d, n_col)}, device_id_type=MESH
        )
    loads = []
    for src, dst in (
        (vel, velv), (vort, vortv), (coarse, coarsev), (xt, xtv), (xc, xcv), (tab, tabv),
    ):
        loads.append(pltpu.make_async_copy(src, dst, load_sem.at[len(loads)]))
        loads[-1].start()
    for load in loads[:3]:
        load.wait()
    pl.semaphore_wait(barrier, n_row + n_col - 2)

    far = me // 2
    order = [3 * (1 - far), 2 - far, 1 + 4 * far - me, me]
    fine = lax.broadcasted_iota(jnp.int32, (rows, rows // RATIO), 0) // RATIO
    cell = lax.broadcasted_iota(jnp.int32, (rows, rows // RATIO), 1)
    spread = jnp.where(fine == cell, 1.0, 0.0).astype(BF16)

    def xcopy(comp, k, dest):
        return pltpu.make_async_remote_copy(
            src_ref=xsend.at[comp, k],
            dst_ref=xrecv.at[comp, me],
            send_sem=xs_sem.at[comp, k],
            recv_sem=xr_sem.at[comp, me],
            device_id={"row": dest},
            device_id_type=MESH,
        )

    def xbody(comp, carry):
        b, c = lax.rem(comp + 1, 3), lax.rem(comp + 2, 3)

        def piece(i, inner):
            lines = pl.ds(pl.multiple_of(i * 16, 16), 16)
            cross = velv[b, lines, :].astype(F32) * vortv[c, lines, :].astype(F32)
            cross = cross - velv[c, lines, :].astype(F32) * vortv[b, lines, :].astype(F32)
            section[lines, :] = (velv[comp, lines, :].astype(F32) + section_step * cross).astype(BF16)
            return inner

        lax.fori_loop(0, rows // 16, piece, 0)
        repeated[...] = jnp.dot(spread, coarsev[comp], preferred_element_type=F32).astype(BF16)

        @pl.when(comp == 0)
        def _():
            loads[3].wait()
            loads[4].wait()

        for k in range(n_row):
            lines = pl.ds(pl.multiple_of(order[k] * width, 16), width)
            total = lax.dot_general(xtv[lines, :], section[...], NT, preferred_element_type=F32)
            total += lax.dot_general(xcv[lines, :], repeated[...], NT, preferred_element_type=F32)
            if k < n_row - 1:
                xsend[comp, k] = total.astype(BF16)
                xcopy(comp, k, order[k]).start()
            else:
                xrecv[comp, me] = total.astype(BF16)
        return carry

    lax.fori_loop(0, 3, xbody, 0)
    loads[5].wait()

    def ycopy(comp, d):
        dest = lax.rem(mc + d, n_col)
        return pltpu.make_async_remote_copy(
            src_ref=ysend.at[comp, dest],
            dst_ref=yrecv.at[comp, mc],
            send_sem=ys_sem.at[comp, d - 1],
            recv_sem=yr_sem.at[comp, mc],
            device_id={"col": dest},
            device_id_type=MESH,
        )

    def ystage(comp):
        for d in range(1, n_row):
            source = lax.rem(me + d, n_row)
            pltpu.make_async_remote_copy(
                src_ref=xsend.at[comp, 0],
                dst_ref=xrecv.at[comp, source],
                send_sem=xs_sem.at[comp, 0],
                recv_sem=xr_sem.at[comp, source],
                device_id={"row": source},
                device_id_type=MESH,
            ).wait_recv()
        half = width // 2
        a = [xrecv[comp, r, :half, :].astype(F32) for r in range(4)]
        b = [xrecv[comp, r, half:, :].astype(F32) for r in range(4)]
        a02, a13, b02, b13 = a[0] + a[2], a[1] + a[3], b[0] + b[2], b[1] + b[3]
        d02, d13, e02, e13 = a[0] - a[2], a[1] - a[3], b[0] - b[2], b[1] - b[3]
        real = [a02 + a13, d02 + e13, a02 - a13, d02 - e13]
        imag = [b02 + b13, e02 - d13, b02 - b13, e02 + d13]
        results = []
        for q in range(4):
            re, im = real[q].astype(BF16), imag[q].astype(BF16)
            turned = jnp.concatenate(
                [jnp.concatenate([re, im], axis=0), jnp.concatenate([im, -re], axis=0)], axis=1
            )
            results.append(lax.dot_general(tabv[q], turned, NT, preferred_element_type=F32))
        part = ysend.shape[2] // 4
        for d in range(n_col):
            ysend[comp, d] = jnp.concatenate(
                [results[q][d * part : (d + 1) * part] for q in range(4)], axis=0
            ).astype(BF16)
        for d in range(1, n_col):
            ycopy(comp, d).start()
        yrecv[comp, mc] = ysend[comp, mc]

    def zstage(comp):
        for d in range(1, n_col):
            source = lax.rem(mc + d, n_col)
            pltpu.make_async_remote_copy(
                src_ref=ysend.at[comp, source],
                dst_ref=yrecv.at[comp, source],
                send_sem=ys_sem.at[comp, d - 1],
                recv_sem=yr_sem.at[comp, source],
                device_id={"col": source},
                device_id_type=MESH,
            ).wait_recv()
        lines, planes, _ = held.shape
        part = lines // 4
        for blk in range(lines // 16):
            cut = slice(blk * 16, (blk + 1) * 16)
            group = yrecv[comp, :, cut, :].reshape(planes * 16, width)
            mixed = jnp.dot(mix[...], group, preferred_element_type=F32)
            held[cut] = mixed.reshape(16, planes, width)

        def body(s, carry):
            for pair in range(2):
                left = held[2 * pair * part + s]
                right = held[(2 * pair + 1) * part + s]
                lanes = pl.ds(pl.multiple_of((2 * s + pair) * 2 * width, 128), 2 * width)
                done[comp, :, lanes] = jnp.concatenate([left, right], axis=1)
            return carry

        lax.fori_loop(0, part, body, 0, unroll=4)
        pltpu.make_async_copy(done.at[comp], out.at[comp], out_sem.at[comp]).start()

    ystage(0)
    ystage(1)
    zstage(0)
    ystage(2)
    zstage(1)
    zstage(2)
    for comp in range(3):
        pltpu.make_async_copy(done.at[comp], out.at[comp], out_sem.at[comp]).wait()
        for k in range(n_row - 1):
            xcopy(comp, k, order[k]).wait_send()
        for d in range(1, n_col):
            ycopy(comp, d).wait_send()


def all_stages(vel, vort, coarse, xt, xc, tab, mix, n_row, n_col):
    _, rows, points = vel.shape
    width = xt.shape[0] // n_row
    lines = 4 * tab.shape[1] // n_col
    anywhere = pl.BlockSpec(memory_space=pl.ANY)
    dma = pltpu.SemaphoreType.DMA
    return pl.pallas_call(
        all_kernel,
        out_shape=jax.ShapeDtypeStruct((3, n_col, lines * width), F32),
        in_specs=[anywhere] * 6 + [pl.BlockSpec(memory_space=pltpu.VMEM)],
        out_specs=anywhere,
        scratch_shapes=[
            pltpu.VMEM(vel.shape, BF16),
            pltpu.VMEM(vort.shape, BF16),
            pltpu.VMEM(coarse.shape, BF16),
            pltpu.VMEM(xt.shape, BF16),
            pltpu.VMEM(xc.shape, BF16),
            pltpu.VMEM(tab.shape, BF16),
            pltpu.VMEM((rows, points), BF16),
            pltpu.VMEM((rows, points // RATIO), BF16),
            pltpu.VMEM((3, n_row, width, rows), BF16),
            pltpu.VMEM((3, n_row, width, rows), BF16),
            pltpu.VMEM((3, n_col, lines, width), BF16),
            pltpu.VMEM((3, n_col, lines, width), BF16),
            pltpu.VMEM((lines, n_col, width), F32),
            pltpu.VMEM((3, n_col, lines * width), F32),
            dma((6,)),
            dma((3, n_row)),
            dma((3, n_row)),
            dma((3, n_col)),
            dma((3, n_col)),
            dma((3,)),
        ],
        compiler_params=pltpu.CompilerParams(
            collective_id=0, has_side_effects=True, vmem_limit_bytes=60 * 2**20
        ),
        name="all_stages",
    )(vel, vort, coarse, xt, xc, tab, mix)


def coarse_forcing(velocity, eddy_state, eddy_rate, block_owner, block_slot):
    components, depth, rows, points = velocity.shape
    coarse_rows = rows // RATIO
    coarse_cols = points // RATIO
    xweights = x_weights(points, coarse_cols, RATIO)
    local = jnp.einsum(
        "czyn,nx->czyx", velocity, xweights, preferred_element_type=jnp.float32
    ).astype(jnp.bfloat16)
    along = padded_2(local, (("row", 2),), 2 * RATIO)
    yweights = y_weights(coarse_rows, rows + 4 * RATIO, RATIO)
    filtered = jnp.einsum(
        "iy,czyx->czix", yweights, along, preferred_element_type=jnp.float32
    ).astype(jnp.bfloat16)
    ybands = coarse_rows // BY
    xbands = coarse_cols // BX
    count = depth * ybands * xbands
    blocks = filtered.reshape(components, depth, ybands, BY, xbands, BX).transpose(1, 2, 4, 0, 3, 5)
    blocks = blocks.reshape(count, BLKV)
    owners = block_owner.reshape(count)
    slots = block_slot.reshape(count)
    owners_total = lax.axis_size("row")
    every_state, every_rate = (
        lax.all_gather(eddy_state, "row", axis=1, tiled=True),
        lax.all_gather(eddy_rate, "row", axis=1, tiled=True),
    )
    chosen = owners * S + slots
    lookup = (chosen[:, None] == jnp.arange(owners_total * S, dtype=jnp.int32)[None, :]).astype(
        jnp.bfloat16
    )
    state = jnp.dot(lookup, every_state[0], preferred_element_type=jnp.float32)
    rates = jnp.dot(lookup, every_rate[0][:, None], preferred_element_type=jnp.float32)[:, 0]
    forcing_blocks = (rates[:, None] * (state - blocks.astype(jnp.float32))).astype(jnp.bfloat16)
    coarse = forcing_blocks.reshape(depth, ybands, xbands, components, BY, BX).transpose(
        3, 0, 1, 4, 2, 5
    )
    return coarse.reshape(components, coarse_rows, coarse_cols)


def vertical_inverse_np(planes):
    index = np.arange(planes)
    ends = (index == 0) | (index == planes - 1)
    matrix = np.diag(np.where(ends, 1.0 + vertical_step, 1.0 + 2.0 * vertical_step))
    for i in range(planes - 1):
        matrix[i, i + 1] = matrix[i + 1, i] = -vertical_step
    return np.linalg.inv(matrix).astype(np.float32)


def per_device(velocity, vorticity, eddy_state, eddy_rate, block_owner, block_slot):
    components, depth, rows, points = velocity.shape
    n_row, n_col = lax.axis_size("row"), lax.axis_size("col")
    if depth != 1 or not fits(rows, points, n_row, n_col):
        return generic_device(velocity, vorticity, eddy_state, eddy_rate, block_owner, block_slot)
    coarse = coarse_forcing(velocity, eddy_state, eddy_rate, block_owner, block_slot)
    vel = velocity.reshape(components, rows, points)
    vort = vorticity.reshape(components, rows, points)
    xt, xc = (jnp.asarray(t) for t in x_tables_t(points, KXM, n_row))
    tab = jnp.asarray(y_tables_t(rows * n_row, KYM, rows))
    mix = jnp.asarray(
        np.einsum("vz,ts->tvzs", vertical_inverse_np(n_col), np.eye(16))
        .reshape(16 * n_col, n_col * 16)
        .astype(BF16)
    )
    mode_rows = KYM // n_col
    mode_cols = KXM // n_row
    x_wave = lax.axis_index("row") * mode_cols + jnp.arange(mode_cols, dtype=jnp.int32)
    y_wave = lax.axis_index("col") * mode_rows + jnp.arange(mode_rows, dtype=jnp.int32) - KYM // 2
    factor = damping(x_wave, y_wave, NX, NY).reshape(-1)
    mixed = all_stages(vel, vort, coarse, xt, xc, tab, mix, n_row, n_col)
    return mixed * factor[None, None, :]


def solution(mesh):
    return jax.shard_map(
        per_device,
        mesh=mesh,
        in_specs=(
            P(None, "col", "row", None),
            P(None, "col", "row", None),
            P("col", "row", None),
            P("col", "row"),
            P("col", "row", None, None),
            P("col", "row", None),
        ),
        out_specs=P(None, None, ("row", "col")),
        check_vma=False,
    )
```

```python
import math

import jax
import jax.numpy as jnp
import numpy as np
from jax import lax
from jax.experimental import pallas as pl
from jax.experimental.pallas import tpu as pltpu
from jax.sharding import PartitionSpec as P

NX = 2048
NY = 2048
KXM = 640
KYM = 1280
RATIO = 4
BY = 8
BX = 128
S = 16
BLKV = 3072


section_step = 0.5
viscous_step = 0.15
vertical_step = 0.5


def padded_2(cells, sides, width):
    for axis, dim in sides:
        count = lax.axis_size(axis)
        head = lax.slice_in_dim(cells, 0, width, axis=dim)
        tail = lax.slice_in_dim(cells, cells.shape[dim] - width, cells.shape[dim], axis=dim)
        cells = jnp.concatenate(
            [
                lax.ppermute(tail, axis, [(i, (i + 1) % count) for i in range(count)]),
                cells,
                lax.ppermute(head, axis, [((i + 1) % count, i) for i in range(count)]),
            ],
            axis=dim,
        )
    return cells


def gauss_value(position, ratio):
    spread = 4.0 * ratio * ratio
    taps = jnp.arange(5 * ratio).astype(jnp.float32)
    shifted = taps - 2.0 * ratio - (ratio - 1) / 2.0
    total = jnp.sum(jnp.exp(-shifted * shifted / (2.0 * spread)))
    moved = position - 2.0 * ratio - (ratio - 1) / 2.0
    return jnp.exp(-moved * moved / (2.0 * spread)) / total


def x_weights(points, coarse, ratio):
    fine = jnp.arange(points, dtype=jnp.int32)[:, None]
    cells = jnp.arange(coarse, dtype=jnp.int32)[None, :]
    offset = jnp.mod(fine - ratio * cells + 2 * ratio, points)
    value = gauss_value(offset.astype(jnp.float32), ratio)
    return jnp.where(offset < 5 * ratio, value, 0.0).astype(jnp.bfloat16)


def y_weights(coarse, padded, ratio):
    cells = jnp.arange(coarse, dtype=jnp.int32)[:, None]
    fine = jnp.arange(padded, dtype=jnp.int32)[None, :]
    offset = fine - ratio * cells
    value = gauss_value(offset.astype(jnp.float32), ratio)
    return jnp.where((offset >= 0) & (offset < 5 * ratio), value, 0.0).astype(jnp.bfloat16)


def x_table(points, kept):
    fine = jnp.arange(points, dtype=jnp.int32)[:, None]
    column = jnp.arange(2 * kept, dtype=jnp.int32)[None, :]
    phase = jnp.mod(column // 2 * fine, points).astype(jnp.float32) * (2.0 * math.pi / points)
    value = jnp.where(column % 2 == 0, jnp.cos(phase), -jnp.sin(phase))
    return (value / math.sqrt(points)).astype(jnp.bfloat16)


def y_tables(points, kept, first, count):
    fine = jnp.arange(points, dtype=jnp.int32)[:, None]
    wave = jnp.arange(count, dtype=jnp.int32)[None, :] + (first - kept // 2)
    phase = jnp.mod(wave * fine, points).astype(jnp.float32) * (2.0 * math.pi / points)
    scale = 1.0 / math.sqrt(points)
    return (
        (jnp.cos(phase) * scale).astype(jnp.bfloat16),
        (jnp.sin(phase) * scale).astype(jnp.bfloat16),
    )


def vertical_inverse(planes):
    index = jnp.arange(planes)
    ends = (index == 0) | (index == planes - 1)
    diagonal = jnp.where(ends, 1.0 + vertical_step, 1.0 + 2.0 * vertical_step).astype(jnp.float32)
    lower = jnp.where(index == 0, 0.0, -vertical_step).astype(jnp.float32)
    upper = jnp.where(index == planes - 1, 0.0, -vertical_step).astype(jnp.float32)
    return lax.linalg.tridiagonal_solve(lower, diagonal, upper, jnp.eye(planes, dtype=jnp.float32))


def damping(x_wave, y_wave, points_x, points_y):
    angle_x = x_wave.astype(jnp.float32) * (2.0 * math.pi / points_x)
    angle_y = y_wave.astype(jnp.float32) * (2.0 * math.pi / points_y)
    total = (
        angle_y[:, None, None] * angle_y[:, None, None]
        + angle_x[None, None, :] * angle_x[None, None, :]
    )
    return jnp.broadcast_to(jnp.exp(-viscous_step * total), (y_wave.shape[0], 2, x_wave.shape[0]))


def along_y(piece):
    items, width, length = piece.shape
    half = width // 2
    split = piece.reshape(items, half, 2, length)
    real_in = split[:, :, 0, :]
    imag_in = split[:, :, 1, :]
    block = 256
    outputs = []
    for first in range(0, KYM, block):
        cosine, sine = y_tables(length, KYM, first, block)
        real_out = jnp.einsum(
            "kin,nj->kji", real_in, cosine, preferred_element_type=jnp.float32
        ) + jnp.einsum("kin,nj->kji", imag_in, sine, preferred_element_type=jnp.float32)
        imag_out = jnp.einsum(
            "kin,nj->kji", imag_in, cosine, preferred_element_type=jnp.float32
        ) - jnp.einsum("kin,nj->kji", real_in, sine, preferred_element_type=jnp.float32)
        outputs.append(jnp.concatenate([real_out, imag_out], axis=2))
    return jnp.concatenate(outputs, axis=1).astype(jnp.bfloat16)


def generic_device(velocity, vorticity, eddy_state, eddy_rate, block_owner, block_slot):
    components, depth, rows, points = velocity.shape
    coarse_rows = rows // RATIO
    coarse_cols = points // RATIO
    xweights = x_weights(points, coarse_cols, RATIO)
    local = jnp.einsum(
        "czyn,nx->czyx", velocity, xweights, preferred_element_type=jnp.float32
    ).astype(jnp.bfloat16)
    along = padded_2(local, (("row", 2),), 2 * RATIO)
    yweights = y_weights(coarse_rows, rows + 4 * RATIO, RATIO)
    filtered = jnp.einsum(
        "iy,czyx->czix", yweights, along, preferred_element_type=jnp.float32
    ).astype(jnp.bfloat16)
    ybands = coarse_rows // BY
    xbands = coarse_cols // BX
    count = depth * ybands * xbands
    blocks = filtered.reshape(components, depth, ybands, BY, xbands, BX).transpose(1, 2, 4, 0, 3, 5)
    blocks = blocks.reshape(count, BLKV)
    owners = block_owner.reshape(count)
    slots = block_slot.reshape(count)
    owners_total = lax.axis_size("row")
    every_state, every_rate = (
        lax.all_gather(eddy_state, "row", axis=1, tiled=True),
        lax.all_gather(eddy_rate, "row", axis=1, tiled=True),
    )
    chosen = owners * S + slots
    lookup = (chosen[:, None] == jnp.arange(owners_total * S, dtype=jnp.int32)[None, :]).astype(
        jnp.bfloat16
    )
    state = jnp.dot(lookup, every_state[0], preferred_element_type=jnp.float32)
    rates = jnp.dot(lookup, every_rate[0][:, None], preferred_element_type=jnp.float32)[:, 0]
    forcing_blocks = (rates[:, None] * (state - blocks.astype(jnp.float32))).astype(jnp.bfloat16)
    coarse = forcing_blocks.reshape(depth, ybands, xbands, components, BY, BX).transpose(
        3, 0, 1, 4, 2, 5
    )
    coarse = coarse.reshape(components, depth, coarse_rows, coarse_cols).astype(jnp.float32)
    forcing = jnp.repeat(jnp.repeat(coarse, RATIO, axis=2), RATIO, axis=3)
    speed = velocity.astype(jnp.float32)
    spin = vorticity.astype(jnp.float32)
    cross = jnp.stack(
        [
            speed[1] * spin[2] - speed[2] * spin[1],
            speed[2] * spin[0] - speed[0] * spin[2],
            speed[0] * spin[1] - speed[1] * spin[0],
        ],
        axis=0,
    )
    section = (speed + section_step * (cross + forcing)).astype(jnp.bfloat16)
    xtable = x_table(points, KXM)
    spectrum = jnp.einsum(
        "kyn,nm->kmy",
        section.reshape(components * depth, rows, points),
        xtable,
        preferred_element_type=jnp.float32,
    ).astype(jnp.bfloat16)
    ordered = along_y(lax.all_to_all(spectrum, "row", split_axis=1, concat_axis=2, tiled=True))
    ordered = ordered.reshape(components, depth, KYM, -1)
    inverse = vertical_inverse(depth * lax.axis_size("col")).astype(jnp.bfloat16)
    mode_rows = KYM // lax.axis_size("col")
    mode_cols = ordered.shape[3] // 2
    x_wave = lax.axis_index("row") * mode_cols + jnp.arange(mode_cols, dtype=jnp.int32)
    y_wave = lax.axis_index("col") * mode_rows + jnp.arange(mode_rows, dtype=jnp.int32) - KYM // 2
    factor = damping(x_wave, y_wave, NX, NY).reshape(-1)
    piece = lax.all_to_all(ordered, "col", split_axis=2, concat_axis=1, tiled=True)
    items = piece.shape[0]
    flat = piece.reshape(items, piece.shape[1], -1)
    mixed = jnp.einsum("wz,kzl->kwl", inverse, flat, preferred_element_type=jnp.float32)
    return mixed * factor[None, None, :]


MESH = pl.DeviceIdType.MESH
F32 = jnp.float32
BF16 = jnp.bfloat16
YB = 256
NT = (((1,), (1,)), ((), ()))


def fits(rows, points, n_row, n_col):
    mode_cols, mode_rows = KXM // n_row, KYM // n_col
    return (
        n_row == 4
        and rows % YB == 0
        and points % 1024 == 0
        and points >= 2048
        and mode_cols % 16 == 0
        and (2 * mode_cols) % 128 == 64
        and mode_rows % 32 == 0
        and n_col == 8
    )


def x_tables_t(points, kept, n_row):
    per = kept // n_row
    row = np.arange(2 * kept)
    wave = row // (2 * per) * per + row % per
    imag = row // per % 2
    phase = (wave[:, None] * np.arange(points)[None, :]) % points * (2.0 * math.pi / points)
    value = np.where(imag[:, None] == 0, np.cos(phase), -np.sin(phase)) / math.sqrt(points)
    fine = value.astype(BF16)
    coarse = section_step * fine.astype(np.float32).reshape(2 * kept, points // RATIO, RATIO).sum(2)
    return fine, coarse.astype(BF16)


def y_tables_t(points, kept, quarter):
    s = np.arange(kept // 4)
    out = []
    for q in range(4):
        wave = 4 * s + q - kept // 2
        phase = (wave[:, None] * np.arange(quarter)[None, :]) % points * (2.0 * math.pi / points)
        out.append(np.concatenate([np.cos(phase), np.sin(phase)], axis=1) / math.sqrt(points))
    return np.stack(out).astype(BF16)


def all_kernel(
    vel, vort, xt, xc, tab, mix, state, chosen, xw, yw, ytop, ybot, out,
    velv, vortv, coarsev, along, edges, every, xtv, xcv, tabv, section, repeated, xsend, xrecv, ysend, yrecv, held, done,
    load_sem, es_sem, er_sem, ss_sem, sr_sem, xs_sem, xr_sem, ys_sem, yr_sem, out_sem,
):
    me, mc = lax.axis_index("row"), lax.axis_index("col")
    n_row, n_col = 4, yrecv.shape[1]
    _, rows, points = velv.shape
    width = xsend.shape[2]
    barrier = pltpu.get_barrier_semaphore()
    for d in range(1, n_row):
        pl.semaphore_signal(
            barrier, inc=1, device_id={"row": lax.rem(me + d, n_row)}, device_id_type=MESH
        )
    for d in range(1, n_col):
        pl.semaphore_signal(
            barrier, inc=1, device_id={"col": lax.rem(mc + d, n_col)}, device_id_type=MESH
        )
    loads = []
    for src, dst in (
        (vel, velv), (vort, vortv), (xt, xtv), (xc, xcv), (tab, tabv),
    ):
        loads.append(pltpu.make_async_copy(src, dst, load_sem.at[len(loads)]))
        loads[-1].start()
    pl.semaphore_wait(barrier, n_row + n_col - 2)

    def scopy(d):
        return pltpu.make_async_remote_copy(
            src_ref=state,
            dst_ref=every.at[:, me],
            send_sem=ss_sem.at[d - 1],
            recv_sem=sr_sem.at[me],
            device_id={"row": lax.rem(me + d, n_row)},
            device_id_type=MESH,
        )

    def ecopy(side):
        dest = lax.rem(me + (1 if side == 0 else n_row - 1), n_row)
        lines = slice(rows - 16, rows) if side == 0 else slice(0, 16)
        return pltpu.make_async_remote_copy(
            src_ref=along.at[:, lines, :],
            dst_ref=edges.at[side],
            send_sem=es_sem.at[side],
            recv_sem=er_sem.at[side],
            device_id={"row": dest},
            device_id_type=MESH,
        )

    for d in range(1, n_row):
        scopy(d).start()
    loads[0].wait()
    cells = points // RATIO

    def filter_x(comp, carry):
        for h in range(cells // 256):
            low, high = 256 * RATIO * h - 128, 256 * RATIO * h + 256 * RATIO + 128
            cuts = [(max(low, 0), min(high, points), max(-low, 0))]
            if low < 0:
                cuts.append((points + low, points, 0))
            if high > points:
                cuts.append((0, high - points, points - low))
            total = 0.0
            for start, stop, at in cuts:
                total += jnp.dot(
                    velv[comp, :, start:stop],
                    xw[at : at + stop - start, :],
                    preferred_element_type=F32,
                )
            along[comp, :, 256 * h : 256 * (h + 1)] = total.astype(BF16)
        return carry

    lax.fori_loop(0, 3, filter_x, 0)
    ecopy(0).start()
    ecopy(1).start()
    every[:, me] = state[...]
    for d in range(1, n_row):
        source = lax.rem(me + d, n_row)
        pltpu.make_async_remote_copy(
            src_ref=state,
            dst_ref=every.at[:, source],
            send_sem=ss_sem.at[d - 1],
            recv_sem=sr_sem.at[source],
            device_id={"row": source},
            device_id_type=MESH,
        ).wait_recv()
    ecopy(0).wait_recv()
    ecopy(1).wait_recv()
    slots = every.shape[1] * every.shape[2]
    lows = rows // RATIO
    sides = xw.shape[1] // 2
    smooth = []
    for comp in range(3):
        total = jnp.dot(yw[...], along[comp], preferred_element_type=F32)
        total += jnp.dot(ytop[...], edges[0, comp], preferred_element_type=F32)
        total += jnp.dot(ybot[...], edges[1, comp], preferred_element_type=F32)
        smooth.append(total.astype(BF16).astype(F32))
    deep = lax.broadcasted_iota(jnp.int32, (lows, BY * slots), 1)
    inner = (lax.broadcasted_iota(jnp.int32, (lows, BY * slots), 0) & (BY - 1)) * slots
    flat = lax.broadcasted_iota(jnp.int32, (lows, slots), 1)
    for q in range(cells // BX):
        name = chosen[:, q : q + 1]
        pick = jnp.where(deep == inner + name, 1.0, 0.0).astype(BF16)
        rate = jnp.dot(
            jnp.where(flat == name, 1.0, 0.0).astype(BF16),
            every[3 * BY].reshape(slots, BX),
            preferred_element_type=F32,
        )
        for comp in range(3):
            held_state = jnp.dot(
                pick,
                every[comp * BY : (comp + 1) * BY].reshape(BY * slots, BX),
                preferred_element_type=F32,
            )
            lanes = slice(q * BX, (q + 1) * BX)
            coarsev[comp, :, lanes] = (rate * (held_state - smooth[comp][:, lanes])).astype(BF16)
    loads[1].wait()

    far = me // 2
    order = [3 * (1 - far), 2 - far, 1 + 4 * far - me, me]
    fine = lax.broadcasted_iota(jnp.int32, (rows, rows // RATIO), 0) // RATIO
    cell = lax.broadcasted_iota(jnp.int32, (rows, rows // RATIO), 1)
    spread = jnp.where(fine == cell, 1.0, 0.0).astype(BF16)

    def xcopy(comp, k, dest):
        return pltpu.make_async_remote_copy(
            src_ref=xsend.at[comp, k],
            dst_ref=xrecv.at[comp, me],
            send_sem=xs_sem.at[comp, k],
            recv_sem=xr_sem.at[comp, me],
            device_id={"row": dest},
            device_id_type=MESH,
        )

    def xbody(comp, carry):
        b, c = lax.rem(comp + 1, 3), lax.rem(comp + 2, 3)

        def piece(i, inner):
            lines = pl.ds(pl.multiple_of(i * 16, 16), 16)
            cross = velv[b, lines, :].astype(F32) * vortv[c, lines, :].astype(F32)
            cross = cross - velv[c, lines, :].astype(F32) * vortv[b, lines, :].astype(F32)
            section[lines, :] = (velv[comp, lines, :].astype(F32) + section_step * cross).astype(BF16)
            return inner

        lax.fori_loop(0, rows // 16, piece, 0)
        repeated[...] = jnp.dot(spread, coarsev[comp], preferred_element_type=F32).astype(BF16)

        @pl.when(comp == 0)
        def _():
            loads[2].wait()
            loads[3].wait()

        for k in range(n_row):
            lines = pl.ds(pl.multiple_of(order[k] * width, 16), width)
            total = lax.dot_general(xtv[lines, :], section[...], NT, preferred_element_type=F32)
            total += lax.dot_general(xcv[lines, :], repeated[...], NT, preferred_element_type=F32)
            if k < n_row - 1:
                xsend[comp, k] = total.astype(BF16)
                xcopy(comp, k, order[k]).start()
            else:
                xrecv[comp, me] = total.astype(BF16)
        return carry

    lax.fori_loop(0, 3, xbody, 0)
    loads[4].wait()

    def ycopy(comp, d):
        dest = lax.rem(mc + d, n_col)
        return pltpu.make_async_remote_copy(
            src_ref=ysend.at[comp, dest],
            dst_ref=yrecv.at[comp, mc],
            send_sem=ys_sem.at[comp, d - 1],
            recv_sem=yr_sem.at[comp, mc],
            device_id={"col": dest},
            device_id_type=MESH,
        )

    def ystage(comp):
        for d in range(1, n_row):
            source = lax.rem(me + d, n_row)
            pltpu.make_async_remote_copy(
                src_ref=xsend.at[comp, 0],
                dst_ref=xrecv.at[comp, source],
                send_sem=xs_sem.at[comp, 0],
                recv_sem=xr_sem.at[comp, source],
                device_id={"row": source},
                device_id_type=MESH,
            ).wait_recv()
        half = width // 2
        a = [xrecv[comp, r, :half, :].astype(F32) for r in range(4)]
        b = [xrecv[comp, r, half:, :].astype(F32) for r in range(4)]
        a02, a13, b02, b13 = a[0] + a[2], a[1] + a[3], b[0] + b[2], b[1] + b[3]
        d02, d13, e02, e13 = a[0] - a[2], a[1] - a[3], b[0] - b[2], b[1] - b[3]
        real = [a02 + a13, d02 + e13, a02 - a13, d02 - e13]
        imag = [b02 + b13, e02 - d13, b02 - b13, e02 + d13]
        results = []
        for q in range(4):
            re, im = real[q].astype(BF16), imag[q].astype(BF16)
            turned = jnp.concatenate(
                [jnp.concatenate([re, im], axis=0), jnp.concatenate([im, -re], axis=0)], axis=1
            )
            results.append(lax.dot_general(tabv[q], turned, NT, preferred_element_type=F32))
        part = ysend.shape[2] // 4
        for d in range(n_col):
            ysend[comp, d] = jnp.concatenate(
                [results[q][d * part : (d + 1) * part] for q in range(4)], axis=0
            ).astype(BF16)
        for d in range(1, n_col):
            ycopy(comp, d).start()
        yrecv[comp, mc] = ysend[comp, mc]

    def zstage(comp):
        for d in range(1, n_col):
            source = lax.rem(mc + d, n_col)
            pltpu.make_async_remote_copy(
                src_ref=ysend.at[comp, source],
                dst_ref=yrecv.at[comp, source],
                send_sem=ys_sem.at[comp, d - 1],
                recv_sem=yr_sem.at[comp, source],
                device_id={"col": source},
                device_id_type=MESH,
            ).wait_recv()
        lines, planes, _ = held.shape
        part = lines // 4
        for blk in range(lines // 16):
            cut = slice(blk * 16, (blk + 1) * 16)
            group = yrecv[comp, :, cut, :].reshape(planes * 16, width)
            mixed = jnp.dot(mix[...], group, preferred_element_type=F32)
            held[cut] = mixed.reshape(16, planes, width)

        def body(s, carry):
            for pair in range(2):
                left = held[2 * pair * part + s]
                right = held[(2 * pair + 1) * part + s]
                lanes = pl.ds(pl.multiple_of((2 * s + pair) * 2 * width, 128), 2 * width)
                done[comp, :, lanes] = jnp.concatenate([left, right], axis=1)
            return carry

        lax.fori_loop(0, part, body, 0, unroll=4)
        pltpu.make_async_copy(done.at[comp], out.at[comp], out_sem.at[comp]).start()

    ystage(0)
    ystage(1)
    zstage(0)
    ystage(2)
    zstage(1)
    zstage(2)
    for d in range(1, n_row):
        scopy(d).wait_send()
    ecopy(0).wait_send()
    ecopy(1).wait_send()
    for comp in range(3):
        pltpu.make_async_copy(done.at[comp], out.at[comp], out_sem.at[comp]).wait()
        for k in range(n_row - 1):
            xcopy(comp, k, order[k]).wait_send()
        for d in range(1, n_col):
            ycopy(comp, d).wait_send()


def all_stages(vel, vort, xt, xc, tab, mix, small, n_row, n_col):
    _, rows, points = vel.shape
    cells = points // RATIO
    state = small[0].shape
    width = xt.shape[0] // n_row
    lines = 4 * tab.shape[1] // n_col
    anywhere = pl.BlockSpec(memory_space=pl.ANY)
    dma = pltpu.SemaphoreType.DMA
    return pl.pallas_call(
        all_kernel,
        out_shape=jax.ShapeDtypeStruct((3, n_col, lines * width), F32),
        in_specs=[anywhere] * 5 + [pl.BlockSpec(memory_space=pltpu.VMEM)] * (1 + len(small)),
        out_specs=anywhere,
        scratch_shapes=[
            pltpu.VMEM(vel.shape, BF16),
            pltpu.VMEM(vort.shape, BF16),
            pltpu.VMEM((3, rows // RATIO, cells), BF16),
            pltpu.VMEM((3, rows, cells), BF16),
            pltpu.VMEM((2, 3, 16, cells), BF16),
            pltpu.VMEM((state[0], n_row, state[1], state[2]), BF16),
            pltpu.VMEM(xt.shape, BF16),
            pltpu.VMEM(xc.shape, BF16),
            pltpu.VMEM(tab.shape, BF16),
            pltpu.VMEM((rows, points), BF16),
            pltpu.VMEM((rows, points // RATIO), BF16),
            pltpu.VMEM((3, n_row, width, rows), BF16),
            pltpu.VMEM((3, n_row, width, rows), BF16),
            pltpu.VMEM((3, n_col, lines, width), BF16),
            pltpu.VMEM((3, n_col, lines, width), BF16),
            pltpu.VMEM((lines, n_col, width), F32),
            pltpu.VMEM((3, n_col, lines * width), F32),
            dma((5,)),
            dma((2,)),
            dma((2,)),
            dma((n_row,)),
            dma((n_row,)),
            dma((3, n_row)),
            dma((3, n_row)),
            dma((3, n_col)),
            dma((3, n_col)),
            dma((3,)),
        ],
        compiler_params=pltpu.CompilerParams(
            collective_id=0, has_side_effects=True, vmem_limit_bytes=60 * 2**20
        ),
        name="all_stages",
    )(vel, vort, xt, xc, tab, mix, *small)


def filter_tables(rows):
    taps = np.arange(5 * RATIO) - 2.0 * RATIO - (RATIO - 1) / 2.0
    value = np.exp(-taps * taps / (8.0 * RATIO * RATIO))
    value = value / value.sum()

    def weights(offset):
        inside = (offset >= 0) & (offset < 5 * RATIO)
        return np.where(inside, value[np.clip(offset, 0, 5 * RATIO - 1)], 0.0).astype(BF16)

    fine = np.arange(256 * RATIO + 256)[:, None] - 128
    xw = weights(fine - RATIO * np.arange(256)[None, :] + 2 * RATIO)
    cell = RATIO * np.arange(rows // RATIO)[:, None] - 2 * RATIO
    yw = weights(np.arange(rows)[None, :] - cell)
    edge = np.arange(16)[None, :]
    return xw, yw, weights(edge - 16 - cell), weights(edge + rows - cell)


def vertical_inverse_np(planes):
    index = np.arange(planes)
    ends = (index == 0) | (index == planes - 1)
    matrix = np.diag(np.where(ends, 1.0 + vertical_step, 1.0 + 2.0 * vertical_step))
    for i in range(planes - 1):
        matrix[i, i + 1] = matrix[i + 1, i] = -vertical_step
    return np.linalg.inv(matrix).astype(np.float32)


def per_device(velocity, vorticity, eddy_state, eddy_rate, block_owner, block_slot):
    components, depth, rows, points = velocity.shape
    n_row, n_col = lax.axis_size("row"), lax.axis_size("col")
    if depth != 1 or not fits(rows, points, n_row, n_col):
        return generic_device(velocity, vorticity, eddy_state, eddy_rate, block_owner, block_slot)
    held = eddy_state.shape[1]
    state = eddy_state[0].reshape(held, components * BY, BX).transpose(1, 0, 2)
    rates = jnp.broadcast_to(eddy_rate[0][None, :, None], (1, held, BX))
    chosen = (block_owner.reshape(-1) * S + block_slot.reshape(-1)).reshape(-1, points // (RATIO * BX))
    small = [jnp.concatenate([state, rates], axis=0), jnp.repeat(chosen, BY, axis=0)]
    small += [jnp.asarray(t) for t in filter_tables(rows)]
    vel = velocity.reshape(components, rows, points)
    vort = vorticity.reshape(components, rows, points)
    xt, xc = (jnp.asarray(t) for t in x_tables_t(points, KXM, n_row))
    tab = jnp.asarray(y_tables_t(rows * n_row, KYM, rows))
    mix = jnp.asarray(
        np.einsum("vz,ts->tvzs", vertical_inverse_np(n_col), np.eye(16))
        .reshape(16 * n_col, n_col * 16)
        .astype(BF16)
    )
    mode_rows = KYM // n_col
    mode_cols = KXM // n_row
    x_wave = lax.axis_index("row") * mode_cols + jnp.arange(mode_cols, dtype=jnp.int32)
    y_wave = lax.axis_index("col") * mode_rows + jnp.arange(mode_rows, dtype=jnp.int32) - KYM // 2
    factor = damping(x_wave, y_wave, NX, NY).reshape(-1)
    mixed = all_stages(vel, vort, xt, xc, tab, mix, small, n_row, n_col)
    return mixed * factor[None, None, :]


def solution(mesh):
    return jax.shard_map(
        per_device,
        mesh=mesh,
        in_specs=(
            P(None, "col", "row", None),
            P(None, "col", "row", None),
            P("col", "row", None),
            P("col", "row"),
            P("col", "row", None, None),
            P("col", "row", None),
        ),
        out_specs=P(None, None, ("row", "col")),
        check_vma=False,
    )
```

```python
import math

import jax
import jax.numpy as jnp
import numpy as np
from jax import lax
from jax.experimental import pallas as pl
from jax.experimental.pallas import tpu as pltpu
from jax.sharding import PartitionSpec as P

NX = 2048
NY = 2048
KXM = 640
KYM = 1280
RATIO = 4
BY = 8
BX = 128
S = 16
BLKV = 3072


section_step = 0.5
viscous_step = 0.15
vertical_step = 0.5


def padded_2(cells, sides, width):
    for axis, dim in sides:
        count = lax.axis_size(axis)
        head = lax.slice_in_dim(cells, 0, width, axis=dim)
        tail = lax.slice_in_dim(cells, cells.shape[dim] - width, cells.shape[dim], axis=dim)
        cells = jnp.concatenate(
            [
                lax.ppermute(tail, axis, [(i, (i + 1) % count) for i in range(count)]),
                cells,
                lax.ppermute(head, axis, [((i + 1) % count, i) for i in range(count)]),
            ],
            axis=dim,
        )
    return cells


def gauss_value(position, ratio):
    spread = 4.0 * ratio * ratio
    taps = jnp.arange(5 * ratio).astype(jnp.float32)
    shifted = taps - 2.0 * ratio - (ratio - 1) / 2.0
    total = jnp.sum(jnp.exp(-shifted * shifted / (2.0 * spread)))
    moved = position - 2.0 * ratio - (ratio - 1) / 2.0
    return jnp.exp(-moved * moved / (2.0 * spread)) / total


def x_weights(points, coarse, ratio):
    fine = jnp.arange(points, dtype=jnp.int32)[:, None]
    cells = jnp.arange(coarse, dtype=jnp.int32)[None, :]
    offset = jnp.mod(fine - ratio * cells + 2 * ratio, points)
    value = gauss_value(offset.astype(jnp.float32), ratio)
    return jnp.where(offset < 5 * ratio, value, 0.0).astype(jnp.bfloat16)


def y_weights(coarse, padded, ratio):
    cells = jnp.arange(coarse, dtype=jnp.int32)[:, None]
    fine = jnp.arange(padded, dtype=jnp.int32)[None, :]
    offset = fine - ratio * cells
    value = gauss_value(offset.astype(jnp.float32), ratio)
    return jnp.where((offset >= 0) & (offset < 5 * ratio), value, 0.0).astype(jnp.bfloat16)


def x_table(points, kept):
    fine = jnp.arange(points, dtype=jnp.int32)[:, None]
    column = jnp.arange(2 * kept, dtype=jnp.int32)[None, :]
    phase = jnp.mod(column // 2 * fine, points).astype(jnp.float32) * (2.0 * math.pi / points)
    value = jnp.where(column % 2 == 0, jnp.cos(phase), -jnp.sin(phase))
    return (value / math.sqrt(points)).astype(jnp.bfloat16)


def y_tables(points, kept, first, count):
    fine = jnp.arange(points, dtype=jnp.int32)[:, None]
    wave = jnp.arange(count, dtype=jnp.int32)[None, :] + (first - kept // 2)
    phase = jnp.mod(wave * fine, points).astype(jnp.float32) * (2.0 * math.pi / points)
    scale = 1.0 / math.sqrt(points)
    return (
        (jnp.cos(phase) * scale).astype(jnp.bfloat16),
        (jnp.sin(phase) * scale).astype(jnp.bfloat16),
    )


def vertical_inverse(planes):
    index = jnp.arange(planes)
    ends = (index == 0) | (index == planes - 1)
    diagonal = jnp.where(ends, 1.0 + vertical_step, 1.0 + 2.0 * vertical_step).astype(jnp.float32)
    lower = jnp.where(index == 0, 0.0, -vertical_step).astype(jnp.float32)
    upper = jnp.where(index == planes - 1, 0.0, -vertical_step).astype(jnp.float32)
    return lax.linalg.tridiagonal_solve(lower, diagonal, upper, jnp.eye(planes, dtype=jnp.float32))


def damping(x_wave, y_wave, points_x, points_y):
    angle_x = x_wave.astype(jnp.float32) * (2.0 * math.pi / points_x)
    angle_y = y_wave.astype(jnp.float32) * (2.0 * math.pi / points_y)
    total = (
        angle_y[:, None, None] * angle_y[:, None, None]
        + angle_x[None, None, :] * angle_x[None, None, :]
    )
    return jnp.broadcast_to(jnp.exp(-viscous_step * total), (y_wave.shape[0], 2, x_wave.shape[0]))


def along_y(piece):
    items, width, length = piece.shape
    half = width // 2
    split = piece.reshape(items, half, 2, length)
    real_in = split[:, :, 0, :]
    imag_in = split[:, :, 1, :]
    block = 256
    outputs = []
    for first in range(0, KYM, block):
        cosine, sine = y_tables(length, KYM, first, block)
        real_out = jnp.einsum(
            "kin,nj->kji", real_in, cosine, preferred_element_type=jnp.float32
        ) + jnp.einsum("kin,nj->kji", imag_in, sine, preferred_element_type=jnp.float32)
        imag_out = jnp.einsum(
            "kin,nj->kji", imag_in, cosine, preferred_element_type=jnp.float32
        ) - jnp.einsum("kin,nj->kji", real_in, sine, preferred_element_type=jnp.float32)
        outputs.append(jnp.concatenate([real_out, imag_out], axis=2))
    return jnp.concatenate(outputs, axis=1).astype(jnp.bfloat16)


def generic_device(velocity, vorticity, eddy_state, eddy_rate, block_owner, block_slot):
    components, depth, rows, points = velocity.shape
    coarse_rows = rows // RATIO
    coarse_cols = points // RATIO
    xweights = x_weights(points, coarse_cols, RATIO)
    local = jnp.einsum(
        "czyn,nx->czyx", velocity, xweights, preferred_element_type=jnp.float32
    ).astype(jnp.bfloat16)
    along = padded_2(local, (("row", 2),), 2 * RATIO)
    yweights = y_weights(coarse_rows, rows + 4 * RATIO, RATIO)
    filtered = jnp.einsum(
        "iy,czyx->czix", yweights, along, preferred_element_type=jnp.float32
    ).astype(jnp.bfloat16)
    ybands = coarse_rows // BY
    xbands = coarse_cols // BX
    count = depth * ybands * xbands
    blocks = filtered.reshape(components, depth, ybands, BY, xbands, BX).transpose(1, 2, 4, 0, 3, 5)
    blocks = blocks.reshape(count, BLKV)
    owners = block_owner.reshape(count)
    slots = block_slot.reshape(count)
    owners_total = lax.axis_size("row")
    every_state, every_rate = (
        lax.all_gather(eddy_state, "row", axis=1, tiled=True),
        lax.all_gather(eddy_rate, "row", axis=1, tiled=True),
    )
    chosen = owners * S + slots
    lookup = (chosen[:, None] == jnp.arange(owners_total * S, dtype=jnp.int32)[None, :]).astype(
        jnp.bfloat16
    )
    state = jnp.dot(lookup, every_state[0], preferred_element_type=jnp.float32)
    rates = jnp.dot(lookup, every_rate[0][:, None], preferred_element_type=jnp.float32)[:, 0]
    forcing_blocks = (rates[:, None] * (state - blocks.astype(jnp.float32))).astype(jnp.bfloat16)
    coarse = forcing_blocks.reshape(depth, ybands, xbands, components, BY, BX).transpose(
        3, 0, 1, 4, 2, 5
    )
    coarse = coarse.reshape(components, depth, coarse_rows, coarse_cols).astype(jnp.float32)
    forcing = jnp.repeat(jnp.repeat(coarse, RATIO, axis=2), RATIO, axis=3)
    speed = velocity.astype(jnp.float32)
    spin = vorticity.astype(jnp.float32)
    cross = jnp.stack(
        [
            speed[1] * spin[2] - speed[2] * spin[1],
            speed[2] * spin[0] - speed[0] * spin[2],
            speed[0] * spin[1] - speed[1] * spin[0],
        ],
        axis=0,
    )
    section = (speed + section_step * (cross + forcing)).astype(jnp.bfloat16)
    xtable = x_table(points, KXM)
    spectrum = jnp.einsum(
        "kyn,nm->kmy",
        section.reshape(components * depth, rows, points),
        xtable,
        preferred_element_type=jnp.float32,
    ).astype(jnp.bfloat16)
    ordered = along_y(lax.all_to_all(spectrum, "row", split_axis=1, concat_axis=2, tiled=True))
    ordered = ordered.reshape(components, depth, KYM, -1)
    inverse = vertical_inverse(depth * lax.axis_size("col")).astype(jnp.bfloat16)
    mode_rows = KYM // lax.axis_size("col")
    mode_cols = ordered.shape[3] // 2
    x_wave = lax.axis_index("row") * mode_cols + jnp.arange(mode_cols, dtype=jnp.int32)
    y_wave = lax.axis_index("col") * mode_rows + jnp.arange(mode_rows, dtype=jnp.int32) - KYM // 2
    factor = damping(x_wave, y_wave, NX, NY).reshape(-1)
    piece = lax.all_to_all(ordered, "col", split_axis=2, concat_axis=1, tiled=True)
    items = piece.shape[0]
    flat = piece.reshape(items, piece.shape[1], -1)
    mixed = jnp.einsum("wz,kzl->kwl", inverse, flat, preferred_element_type=jnp.float32)
    return mixed * factor[None, None, :]


MESH = pl.DeviceIdType.MESH
F32 = jnp.float32
BF16 = jnp.bfloat16
YB = 256
NT = (((1,), (1,)), ((), ()))


def fits(rows, points, n_row, n_col):
    mode_cols, mode_rows = KXM // n_row, KYM // n_col
    return (
        n_row == 4
        and rows % YB == 0
        and points % 1024 == 0
        and points >= 2048
        and mode_cols % 16 == 0
        and (2 * mode_cols) % 128 == 64
        and mode_rows % 32 == 0
        and n_col == 8
    )


def x_tables_t(points, kept, n_row):
    per = kept // n_row
    row = np.arange(2 * kept)
    wave = row // (2 * per) * per + row % per
    imag = row // per % 2
    phase = (wave[:, None] * np.arange(points)[None, :]) % points * (2.0 * math.pi / points)
    value = np.where(imag[:, None] == 0, np.cos(phase), -np.sin(phase)) / math.sqrt(points)
    fine = value.astype(BF16)
    coarse = section_step * fine.astype(np.float32).reshape(2 * kept, points // RATIO, RATIO).sum(2)
    return fine, coarse.astype(BF16)


def y_tables_t(points, kept, quarter):
    s = np.arange(kept // 4)
    out = []
    for q in range(4):
        wave = 4 * s + q - kept // 2
        phase = (wave[:, None] * np.arange(quarter)[None, :]) % points * (2.0 * math.pi / points)
        out.append(np.concatenate([np.cos(phase), np.sin(phase)], axis=1) / math.sqrt(points))
    return np.stack(out).astype(BF16)


def all_kernel(
    vel, vort, xt, xc, tab, mix, state, chosen, xw, yw, ytop, ybot, out,
    velv, vortv, coarsev, along, edges, every, picks, rates, xtv, xcv, tabv, section, repeated, xsend, xrecv, ysend, yrecv, held, done,
    load_sem, es_sem, er_sem, ss_sem, sr_sem, xs_sem, xr_sem, ys_sem, yr_sem, out_sem,
):
    me, mc = lax.axis_index("row"), lax.axis_index("col")
    n_row, n_col = 4, yrecv.shape[1]
    _, rows, points = velv.shape
    width = xsend.shape[2]
    barrier = pltpu.get_barrier_semaphore()
    for d in range(1, n_row):
        pl.semaphore_signal(
            barrier, inc=1, device_id={"row": lax.rem(me + d, n_row)}, device_id_type=MESH
        )
    for d in range(1, n_col):
        pl.semaphore_signal(
            barrier, inc=1, device_id={"col": lax.rem(mc + d, n_col)}, device_id_type=MESH
        )
    loads = [
        pltpu.make_async_copy(src, dst, load_sem.at[n])
        for n, (src, dst) in enumerate(
            [
                (vel.at[0], velv.at[0]),
                (vel.at[1], velv.at[1]),
                (vel.at[2], velv.at[2]),
                (vort.at[1], vortv.at[1]),
                (vort.at[2], vortv.at[2]),
                (vort.at[0], vortv.at[0]),
                (xt, xtv),
                (xc, xcv),
                (tab, tabv),
            ]
        )
    ]
    for load in loads[:5]:
        load.start()

    def scopy(d):
        return pltpu.make_async_remote_copy(
            src_ref=state,
            dst_ref=every.at[:, me],
            send_sem=ss_sem.at[d - 1],
            recv_sem=sr_sem.at[me],
            device_id={"row": lax.rem(me + d, n_row)},
            device_id_type=MESH,
        )

    def ecopy(side, comp):
        dest = lax.rem(me + (1 if side == 0 else n_row - 1), n_row)
        lines = slice(rows - 16, rows) if side == 0 else slice(0, 16)
        return pltpu.make_async_remote_copy(
            src_ref=along.at[comp, lines, :],
            dst_ref=edges.at[side, comp],
            send_sem=es_sem.at[side, comp],
            recv_sem=er_sem.at[side, comp],
            device_id={"row": dest},
            device_id_type=MESH,
        )

    cells = points // RATIO

    def filter_x(comp):
        for h in range(cells // 256):
            low, high = 256 * RATIO * h - 128, 256 * RATIO * h + 256 * RATIO + 128
            cuts = [(max(low, 0), min(high, points), max(-low, 0))]
            if low < 0:
                cuts.append((points + low, points, 0))
            if high > points:
                cuts.append((0, high - points, points - low))
            total = 0.0
            for start, stop, at in cuts:
                total += jnp.dot(
                    velv[comp, :, start:stop],
                    xw[at : at + stop - start, :],
                    preferred_element_type=F32,
                )
            along[comp, :, 256 * h : 256 * (h + 1)] = total.astype(BF16)

    loads[0].wait()
    filter_x(0)
    for load in loads[5:]:
        load.start()
    pl.semaphore_wait(barrier, n_row + n_col - 2)
    ecopy(0, 0).start()
    ecopy(1, 0).start()
    for d in range(1, n_row):
        scopy(d).start()
    every[:, me] = state[...]
    for load in loads[1:5]:
        load.wait()
    slots = every.shape[1] * every.shape[2]
    lows = rows // RATIO

    def lookups():
        for d in range(1, n_row):
            source = lax.rem(me + d, n_row)
            pltpu.make_async_remote_copy(
                src_ref=state,
                dst_ref=every.at[:, source],
                send_sem=ss_sem.at[d - 1],
                recv_sem=sr_sem.at[source],
                device_id={"row": source},
                device_id_type=MESH,
            ).wait_recv()
        deep = lax.broadcasted_iota(jnp.int32, (lows, BY * slots), 1)
        inner = (lax.broadcasted_iota(jnp.int32, (lows, BY * slots), 0) & (BY - 1)) * slots
        flat = lax.broadcasted_iota(jnp.int32, (lows, slots), 1)
        for q in range(cells // BX):
            name = chosen[:, q : q + 1]
            picks[q] = jnp.where(deep == inner + name, 1.0, 0.0).astype(BF16)
            rates[:, q * BX : (q + 1) * BX] = jnp.dot(
                jnp.where(flat == name, 1.0, 0.0).astype(BF16),
                every[3 * BY].reshape(slots, BX),
                preferred_element_type=F32,
            )

    def force(comp):
        ecopy(0, comp).wait_recv()
        ecopy(1, comp).wait_recv()
        total = jnp.dot(yw[...], along[comp], preferred_element_type=F32)
        total += jnp.dot(ytop[...], edges[0, comp], preferred_element_type=F32)
        total += jnp.dot(ybot[...], edges[1, comp], preferred_element_type=F32)
        smooth = total.astype(BF16).astype(F32)
        blocks = every[pl.ds(comp * BY, BY)].reshape(BY * slots, BX)
        for q in range(cells // BX):
            lanes = slice(q * BX, (q + 1) * BX)
            found = jnp.dot(picks[q], blocks, preferred_element_type=F32)
            coarsev[comp, :, lanes] = (rates[:, lanes] * (found - smooth[:, lanes])).astype(BF16)

    far = me // 2
    order = [3 * (1 - far), 2 - far, 1 + 4 * far - me, me]
    fine = lax.broadcasted_iota(jnp.int32, (rows, rows // RATIO), 0) // RATIO
    cell = lax.broadcasted_iota(jnp.int32, (rows, rows // RATIO), 1)
    spread = jnp.where(fine == cell, 1.0, 0.0).astype(BF16)

    def xcopy(comp, k, dest):
        return pltpu.make_async_remote_copy(
            src_ref=xsend.at[comp, k],
            dst_ref=xrecv.at[comp, me],
            send_sem=xs_sem.at[comp, k],
            recv_sem=xr_sem.at[comp, me],
            device_id={"row": dest},
            device_id_type=MESH,
        )

    def xbody(comp, carry):
        b, c = lax.rem(comp + 1, 3), lax.rem(comp + 2, 3)

        def piece(i, inner):
            lines = pl.ds(pl.multiple_of(i * 16, 16), 16)
            cross = velv[b, lines, :].astype(F32) * vortv[c, lines, :].astype(F32)
            cross = cross - velv[c, lines, :].astype(F32) * vortv[b, lines, :].astype(F32)
            section[lines, :] = (velv[comp, lines, :].astype(F32) + section_step * cross).astype(BF16)
            return inner

        lax.fori_loop(0, rows // 16, piece, 0)

        @pl.when(comp == 0)
        def _():
            lookups()
            for load in loads[5:8]:
                load.wait()

        force(comp)
        repeated[...] = jnp.dot(spread, coarsev[comp], preferred_element_type=F32).astype(BF16)

        for k in range(n_row):
            lines = pl.ds(pl.multiple_of(order[k] * width, 16), width)
            total = lax.dot_general(xtv[lines, :], section[...], NT, preferred_element_type=F32)
            total += lax.dot_general(xcv[lines, :], repeated[...], NT, preferred_element_type=F32)
            if k < n_row - 1:
                xsend[comp, k] = total.astype(BF16)
                xcopy(comp, k, order[k]).start()
            else:
                xrecv[comp, me] = total.astype(BF16)

        @pl.when(comp < 2)
        def _():
            filter_x(comp + 1)
            ecopy(0, comp + 1).start()
            ecopy(1, comp + 1).start()

        return carry

    lax.fori_loop(0, 3, xbody, 0)
    loads[8].wait()

    def ycopy(comp, d):
        dest = lax.rem(mc + d, n_col)
        return pltpu.make_async_remote_copy(
            src_ref=ysend.at[comp, dest],
            dst_ref=yrecv.at[comp, mc],
            send_sem=ys_sem.at[comp, d - 1],
            recv_sem=yr_sem.at[comp, mc],
            device_id={"col": dest},
            device_id_type=MESH,
        )

    def ystage(comp):
        for d in range(1, n_row):
            source = lax.rem(me + d, n_row)
            pltpu.make_async_remote_copy(
                src_ref=xsend.at[comp, 0],
                dst_ref=xrecv.at[comp, source],
                send_sem=xs_sem.at[comp, 0],
                recv_sem=xr_sem.at[comp, source],
                device_id={"row": source},
                device_id_type=MESH,
            ).wait_recv()
        half = width // 2
        a = [xrecv[comp, r, :half, :].astype(F32) for r in range(4)]
        b = [xrecv[comp, r, half:, :].astype(F32) for r in range(4)]
        a02, a13, b02, b13 = a[0] + a[2], a[1] + a[3], b[0] + b[2], b[1] + b[3]
        d02, d13, e02, e13 = a[0] - a[2], a[1] - a[3], b[0] - b[2], b[1] - b[3]
        real = [a02 + a13, d02 + e13, a02 - a13, d02 - e13]
        imag = [b02 + b13, e02 - d13, b02 - b13, e02 + d13]
        results = []
        for q in range(4):
            re, im = real[q].astype(BF16), imag[q].astype(BF16)
            turned = jnp.concatenate(
                [jnp.concatenate([re, im], axis=0), jnp.concatenate([im, -re], axis=0)], axis=1
            )
            results.append(lax.dot_general(tabv[q], turned, NT, preferred_element_type=F32))
        part = ysend.shape[2] // 4
        for d in range(n_col):
            ysend[comp, d] = jnp.concatenate(
                [results[q][d * part : (d + 1) * part] for q in range(4)], axis=0
            ).astype(BF16)
        for d in range(1, n_col):
            ycopy(comp, d).start()
        yrecv[comp, mc] = ysend[comp, mc]

    def zstage(comp):
        for d in range(1, n_col):
            source = lax.rem(mc + d, n_col)
            pltpu.make_async_remote_copy(
                src_ref=ysend.at[comp, source],
                dst_ref=yrecv.at[comp, source],
                send_sem=ys_sem.at[comp, d - 1],
                recv_sem=yr_sem.at[comp, source],
                device_id={"col": source},
                device_id_type=MESH,
            ).wait_recv()
        lines, planes, _ = held.shape
        part = lines // 4
        for blk in range(lines // 16):
            cut = slice(blk * 16, (blk + 1) * 16)
            group = yrecv[comp, :, cut, :].reshape(planes * 16, width)
            mixed = jnp.dot(mix[...], group, preferred_element_type=F32)
            held[cut] = mixed.reshape(16, planes, width)

        def body(s, carry):
            for pair in range(2):
                left = held[2 * pair * part + s]
                right = held[(2 * pair + 1) * part + s]
                lanes = pl.ds(pl.multiple_of((2 * s + pair) * 2 * width, 128), 2 * width)
                done[comp, :, lanes] = jnp.concatenate([left, right], axis=1)
            return carry

        lax.fori_loop(0, part, body, 0, unroll=4)
        pltpu.make_async_copy(done.at[comp], out.at[comp], out_sem.at[comp]).start()

    ystage(0)
    ystage(1)
    zstage(0)
    ystage(2)
    zstage(1)
    zstage(2)
    for d in range(1, n_row):
        scopy(d).wait_send()
    for comp in range(3):
        ecopy(0, comp).wait_send()
        ecopy(1, comp).wait_send()
        pltpu.make_async_copy(done.at[comp], out.at[comp], out_sem.at[comp]).wait()
        for k in range(n_row - 1):
            xcopy(comp, k, order[k]).wait_send()
        for d in range(1, n_col):
            ycopy(comp, d).wait_send()


def all_stages(vel, vort, xt, xc, tab, mix, small, n_row, n_col):
    _, rows, points = vel.shape
    cells = points // RATIO
    state = small[0].shape
    width = xt.shape[0] // n_row
    lines = 4 * tab.shape[1] // n_col
    anywhere = pl.BlockSpec(memory_space=pl.ANY)
    dma = pltpu.SemaphoreType.DMA
    return pl.pallas_call(
        all_kernel,
        out_shape=jax.ShapeDtypeStruct((3, n_col, lines * width), F32),
        in_specs=[anywhere] * 5 + [pl.BlockSpec(memory_space=pltpu.VMEM)] * (1 + len(small)),
        out_specs=anywhere,
        scratch_shapes=[
            pltpu.VMEM(vel.shape, BF16),
            pltpu.VMEM(vort.shape, BF16),
            pltpu.VMEM((3, rows // RATIO, cells), BF16),
            pltpu.VMEM((3, rows, cells), BF16),
            pltpu.VMEM((2, 3, 16, cells), BF16),
            pltpu.VMEM((state[0], n_row, state[1], state[2]), BF16),
            pltpu.VMEM((cells // BX, rows // RATIO, BY * n_row * state[1]), BF16),
            pltpu.VMEM((rows // RATIO, cells), F32),
            pltpu.VMEM(xt.shape, BF16),
            pltpu.VMEM(xc.shape, BF16),
            pltpu.VMEM(tab.shape, BF16),
            pltpu.VMEM((rows, points), BF16),
            pltpu.VMEM((rows, points // RATIO), BF16),
            pltpu.VMEM((3, n_row, width, rows), BF16),
            pltpu.VMEM((3, n_row, width, rows), BF16),
            pltpu.VMEM((3, n_col, lines, width), BF16),
            pltpu.VMEM((3, n_col, lines, width), BF16),
            pltpu.VMEM((lines, n_col, width), F32),
            pltpu.VMEM((3, n_col, lines * width), F32),
            dma((9,)),
            dma((2, 3)),
            dma((2, 3)),
            dma((n_row,)),
            dma((n_row,)),
            dma((3, n_row)),
            dma((3, n_row)),
            dma((3, n_col)),
            dma((3, n_col)),
            dma((3,)),
        ],
        compiler_params=pltpu.CompilerParams(
            collective_id=0, has_side_effects=True, vmem_limit_bytes=60 * 2**20
        ),
        name="all_stages",
    )(vel, vort, xt, xc, tab, mix, *small)


def filter_tables(rows):
    taps = np.arange(5 * RATIO) - 2.0 * RATIO - (RATIO - 1) / 2.0
    value = np.exp(-taps * taps / (8.0 * RATIO * RATIO))
    value = value / value.sum()

    def weights(offset):
        inside = (offset >= 0) & (offset < 5 * RATIO)
        return np.where(inside, value[np.clip(offset, 0, 5 * RATIO - 1)], 0.0).astype(BF16)

    fine = np.arange(256 * RATIO + 256)[:, None] - 128
    xw = weights(fine - RATIO * np.arange(256)[None, :] + 2 * RATIO)
    cell = RATIO * np.arange(rows // RATIO)[:, None] - 2 * RATIO
    yw = weights(np.arange(rows)[None, :] - cell)
    edge = np.arange(16)[None, :]
    return xw, yw, weights(edge - 16 - cell), weights(edge + rows - cell)


def vertical_inverse_np(planes):
    index = np.arange(planes)
    ends = (index == 0) | (index == planes - 1)
    matrix = np.diag(np.where(ends, 1.0 + vertical_step, 1.0 + 2.0 * vertical_step))
    for i in range(planes - 1):
        matrix[i, i + 1] = matrix[i + 1, i] = -vertical_step
    return np.linalg.inv(matrix).astype(np.float32)


def per_device(velocity, vorticity, eddy_state, eddy_rate, block_owner, block_slot):
    components, depth, rows, points = velocity.shape
    n_row, n_col = lax.axis_size("row"), lax.axis_size("col")
    if depth != 1 or not fits(rows, points, n_row, n_col):
        return generic_device(velocity, vorticity, eddy_state, eddy_rate, block_owner, block_slot)
    held = eddy_state.shape[1]
    state = eddy_state[0].reshape(held, components * BY, BX).transpose(1, 0, 2)
    rates = jnp.broadcast_to(eddy_rate[0][None, :, None], (1, held, BX))
    chosen = (block_owner.reshape(-1) * S + block_slot.reshape(-1)).reshape(-1, points // (RATIO * BX))
    small = [jnp.concatenate([state, rates], axis=0), jnp.repeat(chosen, BY, axis=0)]
    small += [jnp.asarray(t) for t in filter_tables(rows)]
    vel = velocity.reshape(components, rows, points)
    vort = vorticity.reshape(components, rows, points)
    xt, xc = (jnp.asarray(t) for t in x_tables_t(points, KXM, n_row))
    tab = jnp.asarray(y_tables_t(rows * n_row, KYM, rows))
    mix = jnp.asarray(
        np.einsum("vz,ts->tvzs", vertical_inverse_np(n_col), np.eye(16))
        .reshape(16 * n_col, n_col * 16)
        .astype(BF16)
    )
    mode_rows = KYM // n_col
    mode_cols = KXM // n_row
    x_wave = lax.axis_index("row") * mode_cols + jnp.arange(mode_cols, dtype=jnp.int32)
    y_wave = lax.axis_index("col") * mode_rows + jnp.arange(mode_rows, dtype=jnp.int32) - KYM // 2
    factor = damping(x_wave, y_wave, NX, NY).reshape(-1)
    mixed = all_stages(vel, vort, xt, xc, tab, mix, small, n_row, n_col)
    return mixed * factor[None, None, :]


def solution(mesh):
    return jax.shard_map(
        per_device,
        mesh=mesh,
        in_specs=(
            P(None, "col", "row", None),
            P(None, "col", "row", None),
            P("col", "row", None),
            P("col", "row"),
            P("col", "row", None, None),
            P("col", "row", None),
        ),
        out_specs=P(None, None, ("row", "col")),
        check_vma=False,
    )
```

```python
import math

import jax
import jax.numpy as jnp
import numpy as np
from jax import lax
from jax.experimental import pallas as pl
from jax.experimental.pallas import tpu as pltpu
from jax.sharding import PartitionSpec as P

NX = 2048
NY = 2048
KXM = 640
KYM = 1280
RATIO = 4
BY = 8
BX = 128
S = 16
BLKV = 3072


section_step = 0.5
viscous_step = 0.15
vertical_step = 0.5


def padded_2(cells, sides, width):
    for axis, dim in sides:
        count = lax.axis_size(axis)
        head = lax.slice_in_dim(cells, 0, width, axis=dim)
        tail = lax.slice_in_dim(cells, cells.shape[dim] - width, cells.shape[dim], axis=dim)
        cells = jnp.concatenate(
            [
                lax.ppermute(tail, axis, [(i, (i + 1) % count) for i in range(count)]),
                cells,
                lax.ppermute(head, axis, [((i + 1) % count, i) for i in range(count)]),
            ],
            axis=dim,
        )
    return cells


def gauss_value(position, ratio):
    spread = 4.0 * ratio * ratio
    taps = jnp.arange(5 * ratio).astype(jnp.float32)
    shifted = taps - 2.0 * ratio - (ratio - 1) / 2.0
    total = jnp.sum(jnp.exp(-shifted * shifted / (2.0 * spread)))
    moved = position - 2.0 * ratio - (ratio - 1) / 2.0
    return jnp.exp(-moved * moved / (2.0 * spread)) / total


def x_weights(points, coarse, ratio):
    fine = jnp.arange(points, dtype=jnp.int32)[:, None]
    cells = jnp.arange(coarse, dtype=jnp.int32)[None, :]
    offset = jnp.mod(fine - ratio * cells + 2 * ratio, points)
    value = gauss_value(offset.astype(jnp.float32), ratio)
    return jnp.where(offset < 5 * ratio, value, 0.0).astype(jnp.bfloat16)


def y_weights(coarse, padded, ratio):
    cells = jnp.arange(coarse, dtype=jnp.int32)[:, None]
    fine = jnp.arange(padded, dtype=jnp.int32)[None, :]
    offset = fine - ratio * cells
    value = gauss_value(offset.astype(jnp.float32), ratio)
    return jnp.where((offset >= 0) & (offset < 5 * ratio), value, 0.0).astype(jnp.bfloat16)


def x_table(points, kept):
    fine = jnp.arange(points, dtype=jnp.int32)[:, None]
    column = jnp.arange(2 * kept, dtype=jnp.int32)[None, :]
    phase = jnp.mod(column // 2 * fine, points).astype(jnp.float32) * (2.0 * math.pi / points)
    value = jnp.where(column % 2 == 0, jnp.cos(phase), -jnp.sin(phase))
    return (value / math.sqrt(points)).astype(jnp.bfloat16)


def y_tables(points, kept, first, count):
    fine = jnp.arange(points, dtype=jnp.int32)[:, None]
    wave = jnp.arange(count, dtype=jnp.int32)[None, :] + (first - kept // 2)
    phase = jnp.mod(wave * fine, points).astype(jnp.float32) * (2.0 * math.pi / points)
    scale = 1.0 / math.sqrt(points)
    return (
        (jnp.cos(phase) * scale).astype(jnp.bfloat16),
        (jnp.sin(phase) * scale).astype(jnp.bfloat16),
    )


def vertical_inverse(planes):
    index = jnp.arange(planes)
    ends = (index == 0) | (index == planes - 1)
    diagonal = jnp.where(ends, 1.0 + vertical_step, 1.0 + 2.0 * vertical_step).astype(jnp.float32)
    lower = jnp.where(index == 0, 0.0, -vertical_step).astype(jnp.float32)
    upper = jnp.where(index == planes - 1, 0.0, -vertical_step).astype(jnp.float32)
    return lax.linalg.tridiagonal_solve(lower, diagonal, upper, jnp.eye(planes, dtype=jnp.float32))


def damping(x_wave, y_wave, points_x, points_y):
    angle_x = x_wave.astype(jnp.float32) * (2.0 * math.pi / points_x)
    angle_y = y_wave.astype(jnp.float32) * (2.0 * math.pi / points_y)
    total = (
        angle_y[:, None, None] * angle_y[:, None, None]
        + angle_x[None, None, :] * angle_x[None, None, :]
    )
    return jnp.broadcast_to(jnp.exp(-viscous_step * total), (y_wave.shape[0], 2, x_wave.shape[0]))


def along_y(piece):
    items, width, length = piece.shape
    half = width // 2
    split = piece.reshape(items, half, 2, length)
    real_in = split[:, :, 0, :]
    imag_in = split[:, :, 1, :]
    block = 256
    outputs = []
    for first in range(0, KYM, block):
        cosine, sine = y_tables(length, KYM, first, block)
        real_out = jnp.einsum(
            "kin,nj->kji", real_in, cosine, preferred_element_type=jnp.float32
        ) + jnp.einsum("kin,nj->kji", imag_in, sine, preferred_element_type=jnp.float32)
        imag_out = jnp.einsum(
            "kin,nj->kji", imag_in, cosine, preferred_element_type=jnp.float32
        ) - jnp.einsum("kin,nj->kji", real_in, sine, preferred_element_type=jnp.float32)
        outputs.append(jnp.concatenate([real_out, imag_out], axis=2))
    return jnp.concatenate(outputs, axis=1).astype(jnp.bfloat16)


def generic_device(velocity, vorticity, eddy_state, eddy_rate, block_owner, block_slot):
    components, depth, rows, points = velocity.shape
    coarse_rows = rows // RATIO
    coarse_cols = points // RATIO
    xweights = x_weights(points, coarse_cols, RATIO)
    local = jnp.einsum(
        "czyn,nx->czyx", velocity, xweights, preferred_element_type=jnp.float32
    ).astype(jnp.bfloat16)
    along = padded_2(local, (("row", 2),), 2 * RATIO)
    yweights = y_weights(coarse_rows, rows + 4 * RATIO, RATIO)
    filtered = jnp.einsum(
        "iy,czyx->czix", yweights, along, preferred_element_type=jnp.float32
    ).astype(jnp.bfloat16)
    ybands = coarse_rows // BY
    xbands = coarse_cols // BX
    count = depth * ybands * xbands
    blocks = filtered.reshape(components, depth, ybands, BY, xbands, BX).transpose(1, 2, 4, 0, 3, 5)
    blocks = blocks.reshape(count, BLKV)
    owners = block_owner.reshape(count)
    slots = block_slot.reshape(count)
    owners_total = lax.axis_size("row")
    every_state, every_rate = (
        lax.all_gather(eddy_state, "row", axis=1, tiled=True),
        lax.all_gather(eddy_rate, "row", axis=1, tiled=True),
    )
    chosen = owners * S + slots
    lookup = (chosen[:, None] == jnp.arange(owners_total * S, dtype=jnp.int32)[None, :]).astype(
        jnp.bfloat16
    )
    state = jnp.dot(lookup, every_state[0], preferred_element_type=jnp.float32)
    rates = jnp.dot(lookup, every_rate[0][:, None], preferred_element_type=jnp.float32)[:, 0]
    forcing_blocks = (rates[:, None] * (state - blocks.astype(jnp.float32))).astype(jnp.bfloat16)
    coarse = forcing_blocks.reshape(depth, ybands, xbands, components, BY, BX).transpose(
        3, 0, 1, 4, 2, 5
    )
    coarse = coarse.reshape(components, depth, coarse_rows, coarse_cols).astype(jnp.float32)
    forcing = jnp.repeat(jnp.repeat(coarse, RATIO, axis=2), RATIO, axis=3)
    speed = velocity.astype(jnp.float32)
    spin = vorticity.astype(jnp.float32)
    cross = jnp.stack(
        [
            speed[1] * spin[2] - speed[2] * spin[1],
            speed[2] * spin[0] - speed[0] * spin[2],
            speed[0] * spin[1] - speed[1] * spin[0],
        ],
        axis=0,
    )
    section = (speed + section_step * (cross + forcing)).astype(jnp.bfloat16)
    xtable = x_table(points, KXM)
    spectrum = jnp.einsum(
        "kyn,nm->kmy",
        section.reshape(components * depth, rows, points),
        xtable,
        preferred_element_type=jnp.float32,
    ).astype(jnp.bfloat16)
    ordered = along_y(lax.all_to_all(spectrum, "row", split_axis=1, concat_axis=2, tiled=True))
    ordered = ordered.reshape(components, depth, KYM, -1)
    inverse = vertical_inverse(depth * lax.axis_size("col")).astype(jnp.bfloat16)
    mode_rows = KYM // lax.axis_size("col")
    mode_cols = ordered.shape[3] // 2
    x_wave = lax.axis_index("row") * mode_cols + jnp.arange(mode_cols, dtype=jnp.int32)
    y_wave = lax.axis_index("col") * mode_rows + jnp.arange(mode_rows, dtype=jnp.int32) - KYM // 2
    factor = damping(x_wave, y_wave, NX, NY).reshape(-1)
    piece = lax.all_to_all(ordered, "col", split_axis=2, concat_axis=1, tiled=True)
    items = piece.shape[0]
    flat = piece.reshape(items, piece.shape[1], -1)
    mixed = jnp.einsum("wz,kzl->kwl", inverse, flat, preferred_element_type=jnp.float32)
    return mixed * factor[None, None, :]


MESH = pl.DeviceIdType.MESH
F32 = jnp.float32
BF16 = jnp.bfloat16
YB = 256
NT = (((1,), (1,)), ((), ()))


def fits(rows, points, n_row, n_col):
    mode_cols, mode_rows = KXM // n_row, KYM // n_col
    return (
        n_row == 4
        and rows % YB == 0
        and points % 1024 == 0
        and points >= 2048
        and mode_cols % 16 == 0
        and (2 * mode_cols) % 128 == 64
        and mode_rows % 32 == 0
        and n_col == 8
    )


def x_tables_t(points, kept, n_row):
    per = kept // n_row
    row = np.arange(2 * kept)
    wave = row // (2 * per) * per + row % per
    imag = row // per % 2
    phase = (wave[:, None] * np.arange(points)[None, :]) % points * (2.0 * math.pi / points)
    value = np.where(imag[:, None] == 0, np.cos(phase), -np.sin(phase)) / math.sqrt(points)
    fine = value.astype(BF16)
    coarse = section_step * fine.astype(np.float32).reshape(2 * kept, points // RATIO, RATIO).sum(2)
    return fine, coarse.astype(BF16)


def y_tables_t(points, kept, quarter):
    s = np.arange(kept // 4)
    out = []
    for q in range(4):
        wave = 4 * s + q - kept // 2
        phase = (wave[:, None] * np.arange(quarter)[None, :]) % points * (2.0 * math.pi / points)
        out.append(np.concatenate([np.cos(phase), np.sin(phase)], axis=1) / math.sqrt(points))
    return np.stack(out).astype(BF16)


def all_kernel(
    vel, vort, xt, xc, tab, mix, eddy, pace, owner, slot, xw, yw, ytop, ybot, out,
    velv, vortv, coarsev, along, edges, every, state, xtv, xcv, tabv, section, repeated, xsend, xrecv, ysend, yrecv, held, done,
    load_sem, es_sem, er_sem, ss_sem, sr_sem, xs_sem, xr_sem, ys_sem, yr_sem, out_sem,
):
    me, mc = lax.axis_index("row"), lax.axis_index("col")
    n_row, n_col = 4, yrecv.shape[1]
    _, rows, points = velv.shape
    width = xsend.shape[2]
    barrier = pltpu.get_barrier_semaphore()
    for d in range(1, n_row):
        pl.semaphore_signal(
            barrier, inc=1, device_id={"row": lax.rem(me + d, n_row)}, device_id_type=MESH
        )
    for d in range(1, n_col):
        pl.semaphore_signal(
            barrier, inc=1, device_id={"col": lax.rem(mc + d, n_col)}, device_id_type=MESH
        )
    loads = []
    for src, dst in (
        (vel, velv), (vort, vortv), (xt, xtv), (xc, xcv), (tab, tabv),
    ):
        loads.append(pltpu.make_async_copy(src, dst, load_sem.at[len(loads)]))
        loads[-1].start()
    for v in range(3 * BY):
        state[v] = eddy[:, v * BX : (v + 1) * BX]
    state[3 * BY] = pace[...]
    pl.semaphore_wait(barrier, n_row + n_col - 2)

    def scopy(d):
        return pltpu.make_async_remote_copy(
            src_ref=state,
            dst_ref=every.at[:, me],
            send_sem=ss_sem.at[d - 1],
            recv_sem=sr_sem.at[me],
            device_id={"row": lax.rem(me + d, n_row)},
            device_id_type=MESH,
        )

    def ecopy(side):
        dest = lax.rem(me + (1 if side == 0 else n_row - 1), n_row)
        lines = slice(rows - 16, rows) if side == 0 else slice(0, 16)
        return pltpu.make_async_remote_copy(
            src_ref=along.at[:, lines, :],
            dst_ref=edges.at[side],
            send_sem=es_sem.at[side],
            recv_sem=er_sem.at[side],
            device_id={"row": dest},
            device_id_type=MESH,
        )

    for d in range(1, n_row):
        scopy(d).start()
    loads[0].wait()
    cells = points // RATIO

    def filter_x(comp, carry):
        for h in range(cells // 256):
            low, high = 256 * RATIO * h - 128, 256 * RATIO * h + 256 * RATIO + 128
            cuts = [(max(low, 0), min(high, points), max(-low, 0))]
            if low < 0:
                cuts.append((points + low, points, 0))
            if high > points:
                cuts.append((0, high - points, points - low))
            total = 0.0
            for start, stop, at in cuts:
                total += jnp.dot(
                    velv[comp, :, start:stop],
                    xw[at : at + stop - start, :],
                    preferred_element_type=F32,
                )
            along[comp, :, 256 * h : 256 * (h + 1)] = total.astype(BF16)
        return carry

    lax.fori_loop(0, 3, filter_x, 0)
    ecopy(0).start()
    ecopy(1).start()
    every[:, me] = state[...]
    for d in range(1, n_row):
        source = lax.rem(me + d, n_row)
        pltpu.make_async_remote_copy(
            src_ref=state,
            dst_ref=every.at[:, source],
            send_sem=ss_sem.at[d - 1],
            recv_sem=sr_sem.at[source],
            device_id={"row": source},
            device_id_type=MESH,
        ).wait_recv()
    ecopy(0).wait_recv()
    ecopy(1).wait_recv()
    slots = every.shape[1] * every.shape[2]
    lows = rows // RATIO
    sides = xw.shape[1] // 2
    smooth = []
    for comp in range(3):
        total = jnp.dot(yw[...], along[comp], preferred_element_type=F32)
        total += jnp.dot(ytop[...], edges[0, comp], preferred_element_type=F32)
        total += jnp.dot(ybot[...], edges[1, comp], preferred_element_type=F32)
        smooth.append(total.astype(BF16).astype(F32))
    deep = lax.broadcasted_iota(jnp.int32, (lows, BY * slots), 1)
    inner = (lax.broadcasted_iota(jnp.int32, (lows, BY * slots), 0) & (BY - 1)) * slots
    flat = lax.broadcasted_iota(jnp.int32, (lows, slots), 1)
    count = owner.shape[1]
    chosen = jnp.broadcast_to((owner[...] * S + slot[...]).astype(F32), (lows, count))
    block = lax.broadcasted_iota(jnp.int32, (lows, count), 1)
    band = lax.broadcasted_iota(jnp.int32, (lows, count), 0) // BY * (cells // BX)
    for q in range(cells // BX):
        name = jnp.sum(jnp.where(block == band + q, chosen, 0.0), axis=1, keepdims=True)
        name = name.astype(jnp.int32)
        pick = jnp.where(deep == inner + name, 1.0, 0.0).astype(BF16)
        rate = jnp.dot(
            jnp.where(flat == name, 1.0, 0.0).astype(BF16),
            every[3 * BY].reshape(slots, BX),
            preferred_element_type=F32,
        )
        for comp in range(3):
            held_state = jnp.dot(
                pick,
                every[comp * BY : (comp + 1) * BY].reshape(BY * slots, BX),
                preferred_element_type=F32,
            )
            lanes = slice(q * BX, (q + 1) * BX)
            coarsev[comp, :, lanes] = (rate * (held_state - smooth[comp][:, lanes])).astype(BF16)
    loads[1].wait()

    far = me // 2
    order = [3 * (1 - far), 2 - far, 1 + 4 * far - me, me]
    fine = lax.broadcasted_iota(jnp.int32, (rows, rows // RATIO), 0) // RATIO
    cell = lax.broadcasted_iota(jnp.int32, (rows, rows // RATIO), 1)
    spread = jnp.where(fine == cell, 1.0, 0.0).astype(BF16)

    def xcopy(comp, k, dest):
        return pltpu.make_async_remote_copy(
            src_ref=xsend.at[comp, k],
            dst_ref=xrecv.at[comp, me],
            send_sem=xs_sem.at[comp, k],
            recv_sem=xr_sem.at[comp, me],
            device_id={"row": dest},
            device_id_type=MESH,
        )

    def xbody(comp, carry):
        b, c = lax.rem(comp + 1, 3), lax.rem(comp + 2, 3)

        def piece(i, inner):
            lines = pl.ds(pl.multiple_of(i * 16, 16), 16)
            cross = velv[b, lines, :].astype(F32) * vortv[c, lines, :].astype(F32)
            cross = cross - velv[c, lines, :].astype(F32) * vortv[b, lines, :].astype(F32)
            section[lines, :] = (velv[comp, lines, :].astype(F32) + section_step * cross).astype(BF16)
            return inner

        lax.fori_loop(0, rows // 16, piece, 0)
        repeated[...] = jnp.dot(spread, coarsev[comp], preferred_element_type=F32).astype(BF16)

        @pl.when(comp == 0)
        def _():
            loads[2].wait()
            loads[3].wait()

        for k in range(n_row):
            lines = pl.ds(pl.multiple_of(order[k] * width, 16), width)
            total = lax.dot_general(xtv[lines, :], section[...], NT, preferred_element_type=F32)
            total += lax.dot_general(xcv[lines, :], repeated[...], NT, preferred_element_type=F32)
            if k < n_row - 1:
                xsend[comp, k] = total.astype(BF16)
                xcopy(comp, k, order[k]).start()
            else:
                xrecv[comp, me] = total.astype(BF16)
        return carry

    lax.fori_loop(0, 3, xbody, 0)
    loads[4].wait()

    def ycopy(comp, d):
        dest = lax.rem(mc + d, n_col)
        return pltpu.make_async_remote_copy(
            src_ref=ysend.at[comp, dest],
            dst_ref=yrecv.at[comp, mc],
            send_sem=ys_sem.at[comp, d - 1],
            recv_sem=yr_sem.at[comp, mc],
            device_id={"col": dest},
            device_id_type=MESH,
        )

    def ystage(comp):
        for d in range(1, n_row):
            source = lax.rem(me + d, n_row)
            pltpu.make_async_remote_copy(
                src_ref=xsend.at[comp, 0],
                dst_ref=xrecv.at[comp, source],
                send_sem=xs_sem.at[comp, 0],
                recv_sem=xr_sem.at[comp, source],
                device_id={"row": source},
                device_id_type=MESH,
            ).wait_recv()
        half = width // 2
        a = [xrecv[comp, r, :half, :].astype(F32) for r in range(4)]
        b = [xrecv[comp, r, half:, :].astype(F32) for r in range(4)]
        a02, a13, b02, b13 = a[0] + a[2], a[1] + a[3], b[0] + b[2], b[1] + b[3]
        d02, d13, e02, e13 = a[0] - a[2], a[1] - a[3], b[0] - b[2], b[1] - b[3]
        real = [a02 + a13, d02 + e13, a02 - a13, d02 - e13]
        imag = [b02 + b13, e02 - d13, b02 - b13, e02 + d13]
        results = []
        for q in range(4):
            re, im = real[q].astype(BF16), imag[q].astype(BF16)
            turned = jnp.concatenate(
                [jnp.concatenate([re, im], axis=0), jnp.concatenate([im, -re], axis=0)], axis=1
            )
            results.append(lax.dot_general(tabv[q], turned, NT, preferred_element_type=F32))
        part = ysend.shape[2] // 4
        for d in range(n_col):
            ysend[comp, d] = jnp.concatenate(
                [results[q][d * part : (d + 1) * part] for q in range(4)], axis=0
            ).astype(BF16)
        for d in range(1, n_col):
            ycopy(comp, d).start()
        yrecv[comp, mc] = ysend[comp, mc]

    def zstage(comp):
        for d in range(1, n_col):
            source = lax.rem(mc + d, n_col)
            pltpu.make_async_remote_copy(
                src_ref=ysend.at[comp, source],
                dst_ref=yrecv.at[comp, source],
                send_sem=ys_sem.at[comp, d - 1],
                recv_sem=yr_sem.at[comp, source],
                device_id={"col": source},
                device_id_type=MESH,
            ).wait_recv()
        lines, planes, _ = held.shape
        part = lines // 4
        for blk in range(lines // 16):
            cut = slice(blk * 16, (blk + 1) * 16)
            group = yrecv[comp, :, cut, :].reshape(planes * 16, width)
            mixed = jnp.dot(mix[...], group, preferred_element_type=F32)
            held[cut] = mixed.reshape(16, planes, width)

        def body(s, carry):
            for pair in range(2):
                left = held[2 * pair * part + s]
                right = held[(2 * pair + 1) * part + s]
                lanes = pl.ds(pl.multiple_of((2 * s + pair) * 2 * width, 128), 2 * width)
                done[comp, :, lanes] = jnp.concatenate([left, right], axis=1)
            return carry

        lax.fori_loop(0, part, body, 0, unroll=4)
        pltpu.make_async_copy(done.at[comp], out.at[comp], out_sem.at[comp]).start()

    ystage(0)
    ystage(1)
    zstage(0)
    ystage(2)
    zstage(1)
    zstage(2)
    for d in range(1, n_row):
        scopy(d).wait_send()
    ecopy(0).wait_send()
    ecopy(1).wait_send()
    for comp in range(3):
        pltpu.make_async_copy(done.at[comp], out.at[comp], out_sem.at[comp]).wait()
        for k in range(n_row - 1):
            xcopy(comp, k, order[k]).wait_send()
        for d in range(1, n_col):
            ycopy(comp, d).wait_send()


def all_stages(vel, vort, xt, xc, tab, mix, small, n_row, n_col):
    _, rows, points = vel.shape
    cells = points // RATIO
    state = (3 * BY + 1, small[0].shape[0], BX)
    width = xt.shape[0] // n_row
    lines = 4 * tab.shape[1] // n_col
    anywhere = pl.BlockSpec(memory_space=pl.ANY)
    dma = pltpu.SemaphoreType.DMA
    return pl.pallas_call(
        all_kernel,
        out_shape=jax.ShapeDtypeStruct((3, n_col, lines * width), F32),
        in_specs=[anywhere] * 5 + [pl.BlockSpec(memory_space=pltpu.VMEM)] * (1 + len(small)),
        out_specs=anywhere,
        scratch_shapes=[
            pltpu.VMEM(vel.shape, BF16),
            pltpu.VMEM(vort.shape, BF16),
            pltpu.VMEM((3, rows // RATIO, cells), BF16),
            pltpu.VMEM((3, rows, cells), BF16),
            pltpu.VMEM((2, 3, 16, cells), BF16),
            pltpu.VMEM((state[0], n_row, state[1], state[2]), BF16),
            pltpu.VMEM(state, BF16),
            pltpu.VMEM(xt.shape, BF16),
            pltpu.VMEM(xc.shape, BF16),
            pltpu.VMEM(tab.shape, BF16),
            pltpu.VMEM((rows, points), BF16),
            pltpu.VMEM((rows, points // RATIO), BF16),
            pltpu.VMEM((3, n_row, width, rows), BF16),
            pltpu.VMEM((3, n_row, width, rows), BF16),
            pltpu.VMEM((3, n_col, lines, width), BF16),
            pltpu.VMEM((3, n_col, lines, width), BF16),
            pltpu.VMEM((lines, n_col, width), F32),
            pltpu.VMEM((3, n_col, lines * width), F32),
            dma((5,)),
            dma((2,)),
            dma((2,)),
            dma((n_row,)),
            dma((n_row,)),
            dma((3, n_row)),
            dma((3, n_row)),
            dma((3, n_col)),
            dma((3, n_col)),
            dma((3,)),
        ],
        compiler_params=pltpu.CompilerParams(
            collective_id=0, has_side_effects=True, vmem_limit_bytes=60 * 2**20
        ),
        name="all_stages",
    )(vel, vort, xt, xc, tab, mix, *small)


def filter_tables(rows):
    taps = np.arange(5 * RATIO) - 2.0 * RATIO - (RATIO - 1) / 2.0
    value = np.exp(-taps * taps / (8.0 * RATIO * RATIO))
    value = value / value.sum()

    def weights(offset):
        inside = (offset >= 0) & (offset < 5 * RATIO)
        return np.where(inside, value[np.clip(offset, 0, 5 * RATIO - 1)], 0.0).astype(BF16)

    fine = np.arange(256 * RATIO + 256)[:, None] - 128
    xw = weights(fine - RATIO * np.arange(256)[None, :] + 2 * RATIO)
    cell = RATIO * np.arange(rows // RATIO)[:, None] - 2 * RATIO
    yw = weights(np.arange(rows)[None, :] - cell)
    edge = np.arange(16)[None, :]
    return xw, yw, weights(edge - 16 - cell), weights(edge + rows - cell)


def vertical_inverse_np(planes):
    index = np.arange(planes)
    ends = (index == 0) | (index == planes - 1)
    matrix = np.diag(np.where(ends, 1.0 + vertical_step, 1.0 + 2.0 * vertical_step))
    for i in range(planes - 1):
        matrix[i, i + 1] = matrix[i + 1, i] = -vertical_step
    return np.linalg.inv(matrix).astype(np.float32)


def per_device(velocity, vorticity, eddy_state, eddy_rate, block_owner, block_slot):
    components, depth, rows, points = velocity.shape
    n_row, n_col = lax.axis_size("row"), lax.axis_size("col")
    if depth != 1 or not fits(rows, points, n_row, n_col):
        return generic_device(velocity, vorticity, eddy_state, eddy_rate, block_owner, block_slot)
    held = eddy_state.shape[1]
    small = [
        eddy_state[0],
        jnp.broadcast_to(eddy_rate[0][:, None], (held, BX)),
        block_owner.reshape(1, -1),
        block_slot.reshape(1, -1),
    ]
    small += [jnp.asarray(t) for t in filter_tables(rows)]
    vel = velocity.reshape(components, rows, points)
    vort = vorticity.reshape(components, rows, points)
    xt, xc = (jnp.asarray(t) for t in x_tables_t(points, KXM, n_row))
    tab = jnp.asarray(y_tables_t(rows * n_row, KYM, rows))
    mix = jnp.asarray(
        np.einsum("vz,ts->tvzs", vertical_inverse_np(n_col), np.eye(16))
        .reshape(16 * n_col, n_col * 16)
        .astype(BF16)
    )
    mode_rows = KYM // n_col
    mode_cols = KXM // n_row
    x_wave = lax.axis_index("row") * mode_cols + jnp.arange(mode_cols, dtype=jnp.int32)
    y_wave = lax.axis_index("col") * mode_rows + jnp.arange(mode_rows, dtype=jnp.int32) - KYM // 2
    factor = damping(x_wave, y_wave, NX, NY).reshape(-1)
    mixed = all_stages(vel, vort, xt, xc, tab, mix, small, n_row, n_col)
    return mixed * factor[None, None, :]


def solution(mesh):
    return jax.shard_map(
        per_device,
        mesh=mesh,
        in_specs=(
            P(None, "col", "row", None),
            P(None, "col", "row", None),
            P("col", "row", None),
            P("col", "row"),
            P("col", "row", None, None),
            P("col", "row", None),
        ),
        out_specs=P(None, None, ("row", "col")),
        check_vma=False,
    )
```
